32 devices in a mesh: img: 8 (over z, y), ori: 4 (over x, core).
Axes of the slice: x: 2, y: 2, z: 4, core: 2. Of those that a mesh axis runs over, the one named last changes fastest.
Arguments:
- images: bfloat16 [8192, 4096], P('img'), may hold values from -34 to 34
- img_scale: float32 [8192], P('img'), may hold values from 0.5 to 2
- references: bfloat16 [2048, 4096], P('ori', 'img'), may hold values from -4 to 4
- pattern: int32 [8192, 8], P('img', 'ori'), may hold values from 0 to 1, as said below
- tile_owner: int32 [4, 16384, 1], P('ori', 'img'), may hold values from 0 to 7; in each aligned block of 2048 rows (0 to 2047, 2048 to 4095, ..., all dimensions but the last counted through in order) at most 768 rows name the same one
- tile_brick: int32 [4, 16384], P('ori', 'img'), may hold values from 0 to 15
- tile_block: int32 [4, 16384], P('ori', 'img'), may hold values from 0 to 7
- distance_weights: bfloat16 [8, 128, 512], replicated, may hold values from -0.0234375 to 0.0234375
Outputs:
- bricks: float32 [128, 512], P(('img', 'ori'))
- log_evidence: float32 [8192], P('img')
The draws below stay inside these ranges and needn't reach their ends.
Inputs may be any that keep to these rules, and one draw needn't show every extreme that they name: `pattern`: each image has at least one orientation group set. `tile_owner`: among the 2048 tiles of each aligned block, at most 768 name the same owner, and some block reaches 768.
All inputs are finite; a program needn't handle non-finite values.
Results may differ from the reference program's by a relative error of at most 0.002.
Values may be sent and summed in bfloat16 or wider, within the bound.
A program may use at most 128 MiB of HBM per device.

```python
import math
import jax
import jax.numpy as jnp
import numpy as np
from jax import lax

F = 4096
TS = 128
GROUP = 256
NGROUP = 8
VOX = 512
NPOS = 8
IMG_DEV = 1024
BRICK_DEV = 16
NIMG = 8192
NREF = 2048
TPR = 32
TILES_ORI = 16384
TILES_DEV = 2048
CAP = 768
NBRICK = 128
FAN = 65536
N_IMG = 8
N_ORI = 4


def shared_refs(key):
    return jax.random.truncated_normal(jax.random.fold_in(key, 11), -4.0, 4.0, (NREF, F), jnp.float32)


def forced_group(key):
    return jax.random.randint(jax.random.fold_in(key, 12), (NIMG,), 0, NGROUP)


def draw_references(key, part):
    return shared_refs(key).astype(jnp.bfloat16)


def draw_pattern(key, part):
    coin_flips = jax.random.randint(jax.random.fold_in(key, 15), (NIMG, NGROUP), 0, 2)
    forced = (jnp.arange(NGROUP)[None, :] == forced_group(key)[:, None]).astype(jnp.int32)
    return jnp.maximum(coin_flips, forced)


def draw_images(key, part):
    noise_field = jax.random.truncated_normal(jax.random.fold_in(key, 13), -5.0, 5.0, (NIMG, F), jnp.float32)
    return noise_field.astype(jnp.bfloat16)


def place_ends(drawn, stream_key, smallest, top_value):
    extent = drawn.shape
    place = [jax.random.randint(jax.random.fold_in(stream_key, axis), (), 0, extent[axis]) for axis in range(len(extent))]
    drawn = drawn.at[tuple(place)].set(smallest)
    longest = extent.index(max(extent))
    place[longest] = (place[longest] + 1) % extent[longest]
    return drawn.at[tuple(place)].set(top_value)


def steps_of(stream_key, extent, cuts, least, high):
    factor_of = 1.0
    for axis_at, blocks in cuts:
        steps = jax.random.uniform(jax.random.fold_in(jax.random.fold_in(stream_key, 6), axis_at), (blocks,), jnp.float32, least / len(cuts), high / len(cuts))
        factor_of = factor_of * jnp.repeat(jnp.exp(steps), extent[axis_at] // blocks).reshape((-1,) + (1,) * (len(extent) - 1 - axis_at))
    return factor_of


def deal_out(key, own, number, rows, number_of, top, bound, lean):
    sequence = jax.random.permutation(key, number_of)
    heavy_load, ordinary = load_shares(number_of, rows * top, bound, lean, True), load_shares(number_of, rows * top, bound, lean, False)
    places = jnp.arange(number_of)

    def named(sizes, turn):
        used = int((sizes > 0).sum())
        fixed = max(1, used // 4)
        passed = fixed + (places - fixed + turn * (used - fixed)) % max(1, number_of - fixed)
        return jnp.zeros((number_of,), jnp.int32).at[sequence[jnp.where(places < fixed, places, passed)]].set(jnp.asarray(sizes, jnp.int32))

    sizes = jnp.where(number % 4 == 0, named(heavy_load, number // 4), named(ordinary, number - number // 4 - 1))
    mixed = jax.random.permutation(jax.random.fold_in(own, 3), number_of)
    giver, receiver = mixed[0:number_of // 2 * 2:2], mixed[1:number_of // 2 * 2:2]
    room = jnp.minimum(sizes[giver] - 1, bound - sizes[receiver]) // 2
    room = jnp.where((giver == sequence[0]) | (receiver == sequence[0]) | (sizes[receiver] == 0), 0, jnp.maximum(room, 0))
    passed = jax.random.randint(jax.random.fold_in(own, 4), (number_of // 2,), 0, 1 << 20) % (room + 1)
    sizes = sizes.at[giver].add(-passed).at[receiver].add(passed)
    members = jnp.searchsorted(jnp.cumsum(sizes), jnp.arange(rows * top), side="right").astype(jnp.int32)
    grid = members.reshape(top, rows).T
    grid = grid[jax.random.permutation(jax.random.fold_in(own, 1), rows)]
    turn = jax.random.randint(jax.random.fold_in(own, 2), (rows, 1), 0, top)
    return jnp.take_along_axis(grid, (jnp.arange(top)[None, :] + turn) % top, axis=1)


def load_shares(count, total, bound, skew, full):
    weights = [(1 << 20) // math.isqrt(grade ** skew) + 1 for grade in range(1, count + 1)]
    largest = bound if full else min(bound, max(-(-total // count), total * weights[0] // sum(weights)))
    least = 1 if total - largest >= count - 1 else 0
    counts, rest = [largest] + [least] * (count - 1), total - largest - least * (count - 1)
    while rest > 0:
        free = [i for i in range(1, count) if counts[i] < largest] or [i for i in range(1, count) if counts[i] < bound]
        whole, left = sum([weights[i] for i in free]), rest
        for i in free:
            more = min(bound - counts[i], max(1, left * weights[i] // whole), rest)
            counts[i] = counts[i] + more
            rest = rest - more
    return np.array(counts)


def normal_values(own_key, dims, spread, bound, kind=jnp.bfloat16):
    return jnp.clip(spread * jax.random.normal(own_key, dims, jnp.float32), -bound, bound).astype(kind)


def setup_inputs(seed: int = 0) -> dict:
    arg_keys = jax.random.split(jax.random.key(seed), 9)
    images = draw_images(jax.random.fold_in(arg_keys[8], 71), 0)
    img_scale = jnp.clip(jnp.exp(math.log(2.0) - 1.3862944 * jax.random.uniform(arg_keys[1], (NIMG,), jnp.float32) ** steps_of(arg_keys[1], (NIMG,), ((0, 8),), -0.2, 0.2)), 0.5, 2.0)
    references = draw_references(jax.random.fold_in(arg_keys[8], 71), 0)
    pattern = draw_pattern(jax.random.fold_in(arg_keys[8], 71), 0)
    tile_owner_keys = jax.random.split(jax.random.fold_in(arg_keys[4], 1), N_ORI * TILES_ORI // TILES_DEV)
    tile_owner_turns = jax.random.permutation(jax.random.fold_in(arg_keys[4], 3), N_ORI * TILES_ORI // TILES_DEV)
    tile_owner = jax.vmap(lambda own, number: deal_out(jax.random.fold_in(arg_keys[4], 2), own, number, TILES_DEV, N_IMG, 1, CAP, 2))(tile_owner_keys, tile_owner_turns).reshape((N_ORI, TILES_ORI, 1))
    tile_brick = place_ends(jax.random.randint(arg_keys[5], (N_ORI, TILES_ORI), 0, BRICK_DEV), jax.random.fold_in(arg_keys[5], 1), 0, BRICK_DEV - 1).astype(jnp.int32)
    tile_block = place_ends(jax.random.randint(arg_keys[6], (N_ORI, TILES_ORI), 0, NPOS), jax.random.fold_in(arg_keys[6], 1), 0, NPOS - 1).astype(jnp.int32)
    distance_weights = normal_values(arg_keys[7], (NPOS, TS, VOX), FAN ** -0.5, 0.0234375)
    return {"images": images, "img_scale": img_scale, "references": references, "pattern": pattern, "tile_owner": tile_owner, "tile_brick": tile_brick, "tile_block": tile_block, "distance_weights": distance_weights}


def reference(images, img_scale, references, pattern, tile_owner, tile_brick, tile_block, distance_weights):
    inv_root = 1.0 / math.sqrt(F)
    image_blocks = images.reshape(NIMG // IMG_DEV, IMG_DEV, F)
    scale_blocks = img_scale.reshape(NIMG // IMG_DEV, IMG_DEV)
    flag_blocks = pattern.reshape(NIMG // IMG_DEV, IMG_DEV, NGROUP)

    def visit(totals, block):
        pixels, scales, flags = block
        raw_scores = jnp.dot(pixels, references.T, preferred_element_type=jnp.float32)
        scores = raw_scores * scales[:, None] * inv_root
        active = jnp.repeat(flags > 0, GROUP, axis=1)
        masked = jnp.where(active, scores, -1e+30)
        peak = lax.optimization_barrier(jnp.max(masked, axis=1))
        expo = jnp.where(active, jnp.exp(masked - peak[:, None]), 0.0)
        mass = lax.optimization_barrier(jnp.sum(expo, axis=1))
        weights = expo / mass[:, None]
        scaled = (weights * scales[:, None]).astype(jnp.bfloat16)
        totals = totals + jnp.dot(scaled.T, pixels, preferred_element_type=jnp.float32)
        return (totals, peak + jnp.log(mass))
    start_sums = jnp.zeros((NREF, F), jnp.float32)
    class_sums, evidence = lax.scan(visit, start_sums, (image_blocks, scale_blocks, flag_blocks))
    log_evidence = evidence.reshape(NIMG)
    tiles = class_sums.reshape(NREF * TPR, TS)
    tile_code = ((tile_owner.reshape(-1) * BRICK_DEV + tile_brick.reshape(-1)) * NPOS + tile_block.reshape(-1)).astype(jnp.int32)
    collected = jax.ops.segment_sum(tiles, tile_code, num_segments=NBRICK * NPOS)
    bricks = jnp.einsum('bpt,ptv->bv', collected.reshape(NBRICK, NPOS, TS), distance_weights.astype(jnp.float32), precision=lax.Precision.HIGHEST)
    return (bricks, log_evidence)
```

```python
import functools
import math

import jax
import jax.numpy as jnp
from jax import lax
from jax.experimental import pallas as pl
from jax.experimental.pallas import tpu as pltpu
from jax.sharding import PartitionSpec as P

BRICK_DEV = 16
LANES = 128
NY = 2
PARTS = 2
CORES = 2
PACK = 1 << 16
F8 = jnp.float8_e4m3fn
TOP = 256.0
LOW = 32.0
MESH = pl.DeviceIdType.MESH


def plain_body(
    images, img_scale, references, pattern, tile_owner, tile_brick, tile_block, distance_weights
):
    image_rows, width = images.shape
    ref_local = references.shape[0]
    group_size = ref_local // pattern.shape[1]
    positions, tile_width, voxels = distance_weights.shape
    inv_root = 1.0 / math.sqrt(width)
    weight_table = distance_weights.astype(jnp.float32)
    raw_scores = lax.dot_general(
        images,
        lax.all_gather(references, "img", axis=1, tiled=True),
        (((1,), (1,)), ((), ())),
        preferred_element_type=jnp.float32,
    )
    scores = raw_scores * img_scale[:, None] * inv_root
    active = jnp.repeat(pattern > 0, group_size, axis=1)
    masked = jnp.where(active, scores, -1e30)
    local_peak = jnp.max(masked, axis=1)
    peak = lax.pmax(local_peak, "ori")
    expo = jnp.where(active, jnp.exp(masked - peak[:, None]), 0.0)
    mass = lax.psum(jnp.sum(expo, axis=1), "ori")
    weights = expo / mass[:, None]
    log_evidence = peak + jnp.log(mass)
    scaled = (weights * img_scale[:, None]).astype(jnp.bfloat16)
    partial_value = lax.dot_general(
        scaled, images, (((0,), (0,)), ((), ())), preferred_element_type=jnp.float32
    )
    owners = tile_owner.reshape(-1)
    local_code = tile_brick.reshape(-1) * positions + tile_block.reshape(-1)
    cells = BRICK_DEV * positions
    tile_code = owners * cells + local_code
    group_code = lax.all_gather(tile_code, "img", axis=0, tiled=True)
    peers = lax.axis_size("img")
    group_tiles = partial_value.reshape(-1, tile_width)
    collected = jax.ops.segment_sum(group_tiles, group_code, num_segments=peers * cells)
    brick_terms = jnp.einsum(
        "bpt,ptv->bv",
        collected.reshape(peers * BRICK_DEV, positions, tile_width),
        weight_table,
        precision=lax.Precision.HIGHEST,
    )
    bricks = lax.psum_scatter(brick_terms, ("img", "ori"), scatter_dimension=0, tiled=True)
    return (bricks, log_evidence)


def kernel(
    n_img, n_ori, tiles_ref, inv_root,
    refs, images, scale, pattern, owner, brick_of, block_of, weights,
    sums_out, stats_out,
    img_v, buf, w_v, sc, scaled, codes, codes_buf, codes_all, onehot, rhs, acc,
    halves, stats, stats_buf, terms, terms_buf, mid, mid_buf,
    img_sem, w_sem, own_sem, up_sem, dn_sem, y_sem, recv_sem, code_send, code_recv,
    stat_send, stat_recv, a_send, a_recv, b_send, b_recv, hop_sem,
):
    nz = n_img // NY
    me = lax.axis_index("img")
    ori = lax.axis_index("ori")
    z, y = me // NY, me % NY
    zp = z + 1 - 2 * (z % 2)
    rows, depth = refs.shape
    half = rows // 2
    quarter = rows // PARTS
    n_images = img_v.shape[1]
    groups = pattern.shape[0]
    group = rows // groups
    tile_width, (depth_w, voxels) = acc.shape[1] // 2, w_v.shape
    positions = depth_w // tile_width
    chunk_tiles = depth // tile_width
    cells = acc.shape[0]

    def image_copy(f):
        return pltpu.make_async_copy(
            images.at[:, pl.ds(f * depth, depth)], img_v.at[f], img_sem.at[f]
        )

    for f in range(n_img):
        image_copy(f).start()
    w_copy = pltpu.make_async_copy(weights, w_v, w_sem)
    w_copy.start()

    own_copy = pltpu.make_async_copy(refs, buf.at[me], own_sem)
    own_copy.start()

    up, dn, yn = me + NY, me - NY, z * NY + 1 - y
    has_up, has_dn = z < nz - 1, z > 0
    near = 1 + has_up.astype(jnp.int32) + has_dn.astype(jnp.int32)

    def greet(sem):
        @pl.when(has_up)
        def _():
            pl.semaphore_signal(sem, inc=1, device_id=(up, ori), device_id_type=MESH)

        @pl.when(has_dn)
        def _():
            pl.semaphore_signal(sem, inc=1, device_id=(dn, ori), device_id_type=MESH)

        pl.semaphore_signal(sem, inc=1, device_id=(yn, ori), device_id_type=MESH)

    barrier = pltpu.get_barrier_semaphore()
    greet(barrier)
    for step in range(1, n_ori):
        pl.semaphore_signal(
            barrier, inc=1, device_id=(me, (ori + step) % n_ori), device_id_type=MESH
        )
    per = rows // n_img
    th = tiles_ref // 2
    lines = BRICK_DEV // n_ori
    brick_ids = brick_of[...]
    place_of = brick_ids // lines
    raw = (
        (place_of // CORES) * (cells // (n_ori // CORES))
        + block_of[...] * (CORES * n_img * lines)
        + (place_of % CORES) * (n_img * lines)
        + owner[...] * lines
        + brick_ids % lines
    )
    held_rows = raw.shape[0]
    turned = jnp.concatenate(
        [raw, jnp.zeros((LANES - held_rows, LANES), jnp.int32)], axis=0
    ).T
    local = jnp.zeros((tiles_ref, LANES), jnp.int32)
    for j in range(LANES // tiles_ref):
        cut = turned[j * tiles_ref:(j + 1) * tiles_ref, :]
        local += pltpu.roll(cut, j * held_rows, 1) if j else cut
    wide = local[0:th, :] + pltpu.roll(local[th:, :], per, 1)
    codes[...] = wide[0:th // 2, :] + wide[th // 2:, :] * PACK

    pl.semaphore_wait(barrier, near + n_ori - 1)

    def code_copy(step):
        return pltpu.make_async_remote_copy(
            src_ref=codes,
            dst_ref=codes_buf.at[me],
            send_sem=code_send.at[step],
            recv_sem=code_recv.at[me],
            device_id=((me + step) % n_img, ori),
            device_id_type=MESH,
        )

    def code_arrival(step):
        other = (me + step) % n_img
        return pltpu.make_async_remote_copy(
            src_ref=codes,
            dst_ref=codes_buf.at[other],
            send_sem=code_send.at[step],
            recv_sem=code_recv.at[other],
            device_id=(other, ori),
            device_id_type=MESH,
        )

    def piece(src, sl, q, sems, to):
        return pltpu.make_async_remote_copy(
            src_ref=src,
            dst_ref=buf.at[sl, pl.ds(pl.multiple_of(q * quarter, quarter), quarter), :],
            send_sem=sems.at[sl * PARTS + q],
            recv_sem=recv_sem.at[sl * PARTS + q],
            device_id=(to, ori),
            device_id_type=MESH,
        )

    def held(sl, q):
        return buf.at[sl, pl.ds(pl.multiple_of(q * quarter, quarter), quarter), :]

    for h in range(PARTS):
        own = refs.at[pl.ds(h * quarter, quarter), :]

        @pl.when(has_up)
        def _():
            piece(own, me, h, up_sem, up).start()

        @pl.when(has_dn)
        def _():
            piece(own, me, h, dn_sem, dn).start()

        piece(own, me, h, y_sem, yn).start()

    for hop in range(nz - 1):
        greet(hop_sem.at[hop])
        pl.semaphore_wait(hop_sem.at[hop], near)
    for step in range(1, n_img):
        code_copy(step).start()

    codes_buf[me] = codes[...]
    sc[...] = jnp.zeros_like(sc)
    acc[...] = jnp.zeros_like(acc)
    own_copy.wait()
    for f in range(n_img):
        image_copy(f).wait()

    def brightest(i, top):
        f, at = i // (n_images // 16), pl.multiple_of((i % (n_images // 16)) * 16, 16)
        return jnp.maximum(top, jnp.abs(img_v[f, pl.ds(at, 16), :]))

    bright = lax.fori_loop(
        0, n_img * n_images // 16, brightest, jnp.zeros((16, depth), jnp.bfloat16)
    )
    bright = jnp.max(bright.astype(jnp.float32), axis=(0, 1), keepdims=True)

    def spread_codes():
        for step in range(1, n_img):
            code_arrival(step).wait_recv()
        low = lax.broadcasted_iota(jnp.int32, (th, LANES), 1) < per

        def unpacked(i):
            two = codes_buf[i]
            return jnp.concatenate([two % PACK, two // PACK], axis=0)

        for j in range(n_img // 2):
            a, b = unpacked(2 * j), unpacked(2 * j + 1)
            cut = slice(j * LANES, (j + 1) * LANES)
            codes_all[0:th, cut] = jnp.where(low, a, pltpu.roll(b, per, 1))
            codes_all[th:, cut] = jnp.where(low, pltpu.roll(a, per, 1), b)

    def place(s):
        r, q, k = s // (4 * PARTS), (s // 4) % PARTS, s % 4
        far = q >= PARTS // 2
        other = k // 2
        dist = r - other
        below = (k % 2) == 0
        slz = jnp.where(below, z - dist, z + dist)
        late = jnp.logical_and(jnp.logical_and(r == nz, far), k == 1)
        ok = jnp.logical_and(slz >= 0, slz < nz)
        ok = jnp.logical_and(ok, dist >= jnp.where(below, 0, 1))
        ok = jnp.logical_and(ok, dist < nz)
        skipped = jnp.logical_and(slz == zp, far)
        ok = jnp.logical_and(
            ok, jnp.logical_not(jnp.logical_and(other == 1, skipped))
        )
        ok = jnp.logical_or(ok, late)
        slz = jnp.where(late, zp, slz)
        sl = jnp.where(jnp.logical_or(other == 1, late), slz * NY + 1 - y, slz * NY + y)
        moving = jnp.logical_and(jnp.logical_and(other == 0, r > 0), jnp.logical_not(late))
        moving = jnp.logical_and(moving, ok)
        go_up = jnp.logical_and(jnp.logical_and(moving, below), has_up)
        go_dn = jnp.logical_and(jnp.logical_and(moving, jnp.logical_not(below)), has_dn)
        go_y = jnp.logical_and(moving, jnp.logical_not(skipped))
        sl = jnp.where(ok, sl, me)
        return r, q, k, sl, ok, go_up, go_dn, go_y

    steps = (nz + 1) * 4 * PARTS
    late_sl = z * NY + 1 - y

    strip = 16
    n_strips = half // strip
    factor = scale[...] * inv_root

    blocks = n_images // LANES

    def score_rows(at):
        return jnp.concatenate([sc[c, at, :] for c in range(blocks)], axis=1)

    def keep_rows(at, value):
        for c in range(blocks):
            sc[c, at, :] = value[:, c * LANES:(c + 1) * LANES]

    def half_softmax(h):
        def at_strip(i):
            i = h * n_strips + i
            flag = pattern[pl.ds(i // (group // strip), 1), :] > 0
            return pl.ds(pl.multiple_of(i * strip, strip), strip), flag

        def peak_of(i, m):
            at, flag = at_strip(i)
            s = jnp.where(flag, score_rows(at) * factor, -1e30)
            keep_rows(at, s)
            return jnp.maximum(m, s)

        m = lax.fori_loop(
            0, n_strips, peak_of, jnp.full((strip, n_images), -1e30, jnp.float32)
        )
        m = jnp.max(m, axis=0, keepdims=True)

        def mass_of(i, t):
            at, flag = at_strip(i)
            e = jnp.where(flag, jnp.exp(score_rows(at) - m), 0.0)
            keep_rows(at, e)
            return t + e

        t = lax.fori_loop(0, n_strips, mass_of, jnp.zeros((strip, n_images), jnp.float32))
        halves[2 * h:2 * h + 1, :] = m
        halves[2 * h + 1:2 * h + 2, :] = jnp.sum(t, axis=0, keepdims=True)

    first_hot = 2 * 4 * PARTS

    def arrive(s, carry):
        r, q, k, sl, ok, go_up, go_dn, go_y = place(s)

        @pl.when(s == (nz * PARTS + PARTS // 2) * 4)
        def _():
            half_softmax(0)

        @pl.when(s == first_hot)
        def _():
            spread_codes()

        @pl.when(jnp.logical_and(ok, r + k > 0))
        def _():
            piece(held(sl, q), sl, q, y_sem, yn).wait_recv()

        @pl.when(go_up)
        def _():
            piece(held(sl, q), sl, q, up_sem, up).start()

        @pl.when(go_dn)
        def _():
            piece(held(sl, q), sl, q, dn_sem, dn).start()

        @pl.when(go_y)
        def _():
            piece(held(sl, q), sl, q, y_sem, yn).start()

        turn = jnp.logical_and(r == nz - 1, jnp.logical_and(q == 0, k == 0))

        @pl.when(jnp.logical_and(turn, zp > z))
        def _():
            for late_q in range(PARTS // 2, PARTS):
                piece(held(late_sl, late_q), late_sl, late_q, up_sem, up).start()

        @pl.when(jnp.logical_and(turn, zp < z))
        def _():
            for late_q in range(PARTS // 2, PARTS):
                piece(held(late_sl, late_q), late_sl, late_q, dn_sem, dn).start()

        @pl.when(jnp.logical_and(ok, (q + 1) % (PARTS // 2) == 0))
        def _():
            at = pl.ds(pl.multiple_of((q // (PARTS // 2)) * half, half), half)
            term = lax.dot_general(
                buf[sl, at, :], img_v[sl], (((1,), (1,)), ((), ())),
                preferred_element_type=jnp.float32,
            )
            for c in range(blocks):
                sc[c, at, :] += term[:, c * LANES:(c + 1) * LANES]

        @pl.when(jnp.logical_and(s >= first_hot, s < first_hot + tiles_ref // 2))
        def _():
            for u in range(2):
                tile = 2 * (s - first_hot) + u
                code = codes_all[pl.ds(tile, 1), :]
                f, q = tile // chunk_tiles, tile % chunk_tiles
                at = pl.ds(pl.multiple_of(q * rows, rows), rows)

                def part(i, c):
                    base = pl.multiple_of(i * 64, 64)
                    row = lax.broadcasted_iota(jnp.int32, (64, rows), 0) + base
                    onehot[f, pl.ds(base, 64), at] = jnp.where(row == code, 1.0, 0.0).astype(
                        F8
                    )
                    return c

                lax.fori_loop(0, cells // 64, part, 0)

        return carry

    lax.fori_loop(0, steps, arrive, 0)

    half_softmax(1)
    m = jnp.maximum(halves[0:1, :], halves[2:3, :])
    total = halves[1:2, :] * jnp.exp(halves[0:1, :] - m)
    total += halves[3:4, :] * jnp.exp(halves[2:3, :] - m)
    stats[0:1, :] = m
    stats[1:2, :] = total

    def stat_copy(step, slot):
        return pltpu.make_async_remote_copy(
            src_ref=stats,
            dst_ref=stats_buf.at[slot],
            send_sem=stat_send.at[step],
            recv_sem=stat_recv.at[slot],
            device_id=(me, (ori + step) % n_ori),
            device_id_type=MESH,
        )

    for step in range(1, n_ori):
        stat_copy(step, ori).start()
    peak = m
    for step in range(1, n_ori):
        slot = (ori + step) % n_ori
        stat_copy(step, slot).wait_recv()
        peak = jnp.maximum(peak, stats_buf[slot, 0:1, :])
    mass = total * jnp.exp(m - peak)
    for step in range(1, n_ori):
        slot = (ori + step) % n_ori
        mass += stats_buf[slot, 1:2, :] * jnp.exp(stats_buf[slot, 0:1, :] - peak)
    stats_out[0:1, :] = peak
    stats_out[1:2, :] = mass
    share_of = scale[...] / mass

    spread = LANES // tiles_ref
    power = jnp.zeros((strip, 1), jnp.float32)
    for h in range(2):
        weight = jnp.exp(halves[2 * h:2 * h + 1, :] - peak) * share_of

        def scale_of(i, top):
            i = h * n_strips + i
            first = (i // spread) * per + i % spread
            at = pl.ds(pl.multiple_of(i * strip, strip), strip)
            value = score_rows(pl.ds(first, strip, stride=spread)) * weight
            scaled[at, :] = value.astype(jnp.bfloat16)
            return jnp.maximum(top, jnp.sum(value * value, axis=1, keepdims=True))

        power = lax.fori_loop(0, n_strips, scale_of, power)
    largest = jnp.maximum(jnp.sqrt(jnp.max(power, axis=0, keepdims=True)), 1e-15)
    largest = largest * (math.sqrt(n_images) * jnp.maximum(bright, 1e-18))
    grow, shrink = TOP / largest, largest * (1.0 / TOP)

    def values(f):
        value = jnp.dot(scaled[...], img_v[f], preferred_element_type=jnp.float32) * grow
        hi = value.astype(F8)
        lo = ((value - hi.astype(jnp.float32)) * LOW).astype(F8)
        for q in range(chunk_tiles):
            cut = slice(q * tile_width, (q + 1) * tile_width)
            rhs[f, q * rows:(q + 1) * rows, 0:tile_width] = hi[:, cut]
            rhs[f, q * rows:(q + 1) * rows, tile_width:] = lo[:, cut]

    x_me, core = ori // CORES, ori % CORES
    chips = n_ori // CORES
    side = cells // chips
    share = n_img * lines

    def collect(f, chip):
        at = pl.ds(pl.multiple_of(chip * side, side), side)
        acc[at, :] += jnp.dot(onehot[f, at, :], rhs[f], preferred_element_type=jnp.float32)

    def brick_terms(chip):
        at = pl.ds(pl.multiple_of(chip * side, side), side)
        both = acc[at, :]
        c = (both[:, 0:tile_width] + both[:, tile_width:] * (1.0 / LOW)) * shrink
        hi = c.astype(jnp.bfloat16)
        lo = (c - hi.astype(jnp.float32)).astype(jnp.bfloat16)
        n = side // positions
        wide_hi = jnp.concatenate([hi[p * n:(p + 1) * n, :] for p in range(positions)], axis=1)
        wide_lo = jnp.concatenate([lo[p * n:(p + 1) * n, :] for p in range(positions)], axis=1)
        brick = jnp.dot(wide_hi, w_v[...], preferred_element_type=jnp.float32)
        brick += jnp.dot(wide_lo, w_v[...], preferred_element_type=jnp.float32)
        for c in range(CORES):
            terms[chip * CORES + c] = brick[c * share:(c + 1) * share, :]

    def term_copy(to, slot):
        return pltpu.make_async_remote_copy(
            src_ref=terms.at[to],
            dst_ref=terms_buf.at[slot],
            send_sem=a_send.at[to],
            recv_sem=a_recv.at[slot],
            device_id=(me, to),
            device_id_type=MESH,
        )

    values(0)

    def first_side(f, c):
        values(f + 1)
        collect(f, 1 - x_me)
        return c

    lax.fori_loop(0, n_img - 1, first_side, 0)
    collect(n_img - 1, 1 - x_me)
    w_copy.wait()
    brick_terms(1 - x_me)
    for c in range(CORES):
        term_copy((1 - x_me) * CORES + c, ori).start()

    def second_side(f, c):
        collect(f, x_me)
        return c

    lax.fori_loop(0, n_img, second_side, 0)
    brick_terms(x_me)
    mate = x_me * CORES + 1 - core
    term_copy(mate, ori).start()
    mine = terms[ori]
    term_copy(mate, mate).wait_recv()
    mine += terms_buf[mate]
    for c in range(CORES):
        slot = (1 - x_me) * CORES + c
        term_copy(slot, slot).wait_recv()
        mine += terms_buf[slot]
    for i in range(n_img):
        mid[i] = mine[i * lines:(i + 1) * lines, :]

    def mid_copy(step, slot):
        to = (me + step) % n_img
        return pltpu.make_async_remote_copy(
            src_ref=mid.at[to],
            dst_ref=mid_buf.at[slot],
            send_sem=b_send.at[step],
            recv_sem=b_recv.at[slot],
            device_id=(to, ori),
            device_id_type=MESH,
        )

    for step in range(1, n_img):
        mid_copy(step, me).start()
    for step in range(1, n_img):
        code_copy(step).wait_send()
    for step in range(1, n_ori):
        stat_copy(step, ori).wait_send()
        term_copy((ori + step) % n_ori, ori).wait_send()
    for h in range(PARTS):
        own = refs.at[pl.ds(h * quarter, quarter), :]

        @pl.when(has_up)
        def _():
            piece(own, me, h, up_sem, up).wait_send()

        @pl.when(has_dn)
        def _():
            piece(own, me, h, dn_sem, dn).wait_send()

        piece(own, me, h, y_sem, yn).wait_send()

    @pl.when(zp > z)
    def _():
        for late_q in range(PARTS // 2, PARTS):
            piece(held(late_sl, late_q), late_sl, late_q, up_sem, up).wait_send()

    @pl.when(zp < z)
    def _():
        for late_q in range(PARTS // 2, PARTS):
            piece(held(late_sl, late_q), late_sl, late_q, dn_sem, dn).wait_send()

    def drain(s, carry):
        r, q, k, sl, ok, go_up, go_dn, go_y = place(s)

        @pl.when(go_up)
        def _():
            piece(held(sl, q), sl, q, up_sem, up).wait_send()

        @pl.when(go_dn)
        def _():
            piece(held(sl, q), sl, q, dn_sem, dn).wait_send()

        @pl.when(go_y)
        def _():
            piece(held(sl, q), sl, q, y_sem, yn).wait_send()

        return carry

    lax.fori_loop(0, steps, drain, 0)

    result = mid[me]
    for step in range(1, n_img):
        slot = (me + step) % n_img
        mid_copy(step, slot).wait_recv()
        if step < n_img - 1:
            result += mid_buf[slot]
    sums_out[0] = result
    sums_out[1] = mid_buf[(me + n_img - 1) % n_img]
    for step in range(1, n_img):
        mid_copy(step, me).wait_send()


def finish(sums, stats, bricks, evidence):
    bricks[...] = sums[0] + sums[1]
    evidence[...] = stats[0:1, :] + jnp.log(stats[1:2, :])


def fused_body(
    images, img_scale, references, pattern, tile_owner, tile_brick, tile_block, distance_weights
):
    n_img, n_ori = lax.axis_size("img"), lax.axis_size("ori")
    n_images, width = images.shape
    rows, depth = references.shape
    positions, tile_width, voxels = distance_weights.shape
    tiles_ref = width // tile_width
    lines = BRICK_DEV // n_ori
    cells = n_img * BRICK_DEV * positions
    flat = (tile_brick.size // LANES, LANES)
    bf16, f32, i32 = jnp.bfloat16, jnp.float32, jnp.int32
    vmem = pl.BlockSpec(memory_space=pltpu.VMEM)
    hbm = pl.BlockSpec(memory_space=pl.ANY)
    dma = pltpu.SemaphoreType.DMA
    sums, stats = pl.pallas_call(
        functools.partial(kernel, n_img, n_ori, tiles_ref, 1.0 / math.sqrt(width)),
        out_shape=(
            jax.ShapeDtypeStruct((2, lines, voxels), f32),
            jax.ShapeDtypeStruct((2, n_images), f32),
        ),
        in_specs=[hbm, hbm, vmem, vmem, vmem, vmem, vmem, hbm],
        out_specs=(vmem, vmem),
        scratch_shapes=[
            pltpu.VMEM((n_img, n_images, depth), bf16),
            pltpu.VMEM((n_img, rows, depth), bf16),
            pltpu.VMEM((positions * tile_width, voxels), bf16),
            pltpu.VMEM((n_images // LANES, rows, LANES), f32),
            pltpu.VMEM((rows, n_images), bf16),
            pltpu.VMEM((tiles_ref // 4, LANES), i32),
            pltpu.VMEM((n_img, tiles_ref // 4, LANES), i32),
            pltpu.VMEM((tiles_ref, rows), i32),
            pltpu.VMEM((n_img, cells, rows * depth // tile_width), F8),
            pltpu.VMEM((n_img, rows * depth // tile_width, 2 * tile_width), F8),
            pltpu.VMEM((cells, 2 * tile_width), f32),
            pltpu.VMEM((4, n_images), f32),
            pltpu.VMEM((2, n_images), f32),
            pltpu.VMEM((n_ori, 2, n_images), f32),
            pltpu.VMEM((n_ori, n_img * lines, voxels), f32),
            pltpu.VMEM((n_ori, n_img * lines, voxels), f32),
            pltpu.VMEM((n_img, lines, voxels), f32),
            pltpu.VMEM((n_img, lines, voxels), f32),
            dma((n_img,)),
            dma,
            dma,
            dma((PARTS * n_img,)),
            dma((PARTS * n_img,)),
            dma((PARTS * n_img,)),
            dma((PARTS * n_img,)),
            dma((n_img,)),
            dma((n_img,)),
            dma((n_ori,)),
            dma((n_ori,)),
            dma((n_ori,)),
            dma((n_ori,)),
            dma((n_img,)),
            dma((n_img,)),
            pltpu.SemaphoreType.REGULAR((n_img // NY - 1,)),
        ],
        compiler_params=pltpu.CompilerParams(
            collective_id=0, has_side_effects=True, vmem_limit_bytes=67043328
        ),
    )(
        references,
        images,
        img_scale[None, :],
        pattern.T,
        tile_owner.reshape(flat),
        tile_brick.reshape(flat),
        tile_block.reshape(flat),
        distance_weights.reshape(positions * tile_width, voxels),
    )
    bricks, evidence = pl.pallas_call(
        finish,
        out_shape=(
            jax.ShapeDtypeStruct((lines, voxels), f32),
            jax.ShapeDtypeStruct((1, n_images), f32),
        ),
        in_specs=[vmem, vmem],
        out_specs=(vmem, vmem),
    )(sums, stats)
    return bricks, evidence.reshape(-1)


def body(*args):
    images, references, weights = args[0], args[2], args[7]
    n_img = lax.axis_size("img")
    rows, depth = references.shape
    cells = n_img * BRICK_DEV * weights.shape[0]
    tiles_ref = images.shape[1] // weights.shape[1]
    room = 2 * (images.size + rows * depth * n_img * (1 + cells // weights.shape[1]))
    fits = (
        depth % LANES == 0
        and 2 * (rows // n_img) == LANES
        and LANES % tiles_ref == 0
        and tiles_ref % 32 == 0
        and cells <= PACK // 2
        and lax.axis_size("ori") == 2 * CORES
        and rows * tiles_ref == 16 * LANES * n_img
        and n_img % (2 * NY) == 0
        and n_img >= 4 * NY
        and room < 48 * 2**20
    )
    return fused_body(*args) if fits else plain_body(*args)


def solution(mesh):
    placed = (
        P("img", None),
        P("img"),
        P("ori", "img"),
        P("img", "ori"),
        P("ori", "img", None),
        P("ori", "img"),
        P("ori", "img"),
        P(),
    )
    return jax.shard_map(
        body,
        mesh=mesh,
        in_specs=placed,
        out_specs=(P(("img", "ori"), None), P("img")),
        check_vma=False,
    )
```

```python
import functools
import math

import jax
import jax.numpy as jnp
from jax import lax
from jax.experimental import pallas as pl
from jax.experimental.pallas import tpu as pltpu
from jax.sharding import PartitionSpec as P

BRICK_DEV = 16
LANES = 128
NY = 2
PARTS = 2
CORES = 2
PACK = 1 << 16
F8 = jnp.float8_e4m3fn
TOP = 256.0
LOW = 32.0
MESH = pl.DeviceIdType.MESH


def plain_body(
    images, img_scale, references, pattern, tile_owner, tile_brick, tile_block, distance_weights
):
    image_rows, width = images.shape
    ref_local = references.shape[0]
    group_size = ref_local // pattern.shape[1]
    positions, tile_width, voxels = distance_weights.shape
    inv_root = 1.0 / math.sqrt(width)
    weight_table = distance_weights.astype(jnp.float32)
    raw_scores = lax.dot_general(
        images,
        lax.all_gather(references, "img", axis=1, tiled=True),
        (((1,), (1,)), ((), ())),
        preferred_element_type=jnp.float32,
    )
    scores = raw_scores * img_scale[:, None] * inv_root
    active = jnp.repeat(pattern > 0, group_size, axis=1)
    masked = jnp.where(active, scores, -1e30)
    local_peak = jnp.max(masked, axis=1)
    peak = lax.pmax(local_peak, "ori")
    expo = jnp.where(active, jnp.exp(masked - peak[:, None]), 0.0)
    mass = lax.psum(jnp.sum(expo, axis=1), "ori")
    weights = expo / mass[:, None]
    log_evidence = peak + jnp.log(mass)
    scaled = (weights * img_scale[:, None]).astype(jnp.bfloat16)
    partial_value = lax.dot_general(
        scaled, images, (((0,), (0,)), ((), ())), preferred_element_type=jnp.float32
    )
    owners = tile_owner.reshape(-1)
    local_code = tile_brick.reshape(-1) * positions + tile_block.reshape(-1)
    cells = BRICK_DEV * positions
    tile_code = owners * cells + local_code
    group_code = lax.all_gather(tile_code, "img", axis=0, tiled=True)
    peers = lax.axis_size("img")
    group_tiles = partial_value.reshape(-1, tile_width)
    collected = jax.ops.segment_sum(group_tiles, group_code, num_segments=peers * cells)
    brick_terms = jnp.einsum(
        "bpt,ptv->bv",
        collected.reshape(peers * BRICK_DEV, positions, tile_width),
        weight_table,
        precision=lax.Precision.HIGHEST,
    )
    bricks = lax.psum_scatter(brick_terms, ("img", "ori"), scatter_dimension=0, tiled=True)
    return (bricks, log_evidence)


def kernel(
    n_img, n_ori, tiles_ref, inv_root,
    refs, images, scale, pattern, owner, brick_of, block_of, weights,
    sums_out, stats_out,
    img_v, buf, w_v, sc, scaled, codes, codes_buf, codes_all, onehot, rhs_a, rhs_b, acc,
    halves, stats, stats_buf, terms, terms_buf, mid, mid_buf,
    img_sem, w_sem, own_sem, up_sem, dn_sem, y_sem, recv_sem, code_send, code_recv,
    stat_send, stat_recv, a_send, a_recv, b_send, b_recv, hop_sem,
):
    nz = n_img // NY
    me = lax.axis_index("img")
    ori = lax.axis_index("ori")
    z, y = me // NY, me % NY
    zp = z + 1 - 2 * (z % 2)
    rows, depth = refs.shape
    half = rows // 2
    quarter = rows // PARTS
    n_images = img_v.shape[1]
    groups = pattern.shape[0]
    group = rows // groups
    tile_width, (depth_w, voxels) = acc.shape[1] // 2, w_v.shape
    positions = depth_w // tile_width
    chunk_tiles = depth // tile_width
    cells = acc.shape[0]

    def image_copy(f):
        return pltpu.make_async_copy(
            images.at[:, pl.ds(f * depth, depth)], img_v.at[f], img_sem.at[f]
        )

    w_copy = pltpu.make_async_copy(weights, w_v, w_sem)
    own_copy = pltpu.make_async_copy(refs, buf.at[me], own_sem)

    up, dn, yn = me + NY, me - NY, z * NY + 1 - y
    has_up, has_dn = z < nz - 1, z > 0
    near = 1 + has_up.astype(jnp.int32) + has_dn.astype(jnp.int32)

    def greet(sem):
        @pl.when(has_up)
        def _():
            pl.semaphore_signal(sem, inc=1, device_id=(up, ori), device_id_type=MESH)

        @pl.when(has_dn)
        def _():
            pl.semaphore_signal(sem, inc=1, device_id=(dn, ori), device_id_type=MESH)

        pl.semaphore_signal(sem, inc=1, device_id=(yn, ori), device_id_type=MESH)

    barrier = pltpu.get_barrier_semaphore()
    greet(barrier)
    for step in range(1, n_ori):
        pl.semaphore_signal(
            barrier, inc=1, device_id=(me, (ori + step) % n_ori), device_id_type=MESH
        )
    per = rows // n_img
    th = tiles_ref // 2
    lines = BRICK_DEV // n_ori
    brick_ids = brick_of[...]
    place_of = brick_ids // lines
    raw = (
        (place_of // CORES) * (cells // (n_ori // CORES))
        + block_of[...] * (CORES * n_img * lines)
        + (place_of % CORES) * (n_img * lines)
        + owner[...] * lines
        + brick_ids % lines
    )
    held_rows = raw.shape[0]
    turned = jnp.concatenate(
        [raw, jnp.zeros((LANES - held_rows, LANES), jnp.int32)], axis=0
    ).T
    local = jnp.zeros((tiles_ref, LANES), jnp.int32)
    for j in range(LANES // tiles_ref):
        cut = turned[j * tiles_ref:(j + 1) * tiles_ref, :]
        local += pltpu.roll(cut, j * held_rows, 1) if j else cut
    wide = local[0:th, :] + pltpu.roll(local[th:, :], per, 1)
    codes[...] = wide[0:th // 2, :] + wide[th // 2:, :] * PACK

    pl.semaphore_wait(barrier, near + n_ori - 1)

    def code_copy(step):
        return pltpu.make_async_remote_copy(
            src_ref=codes,
            dst_ref=codes_buf.at[me],
            send_sem=code_send.at[step],
            recv_sem=code_recv.at[me],
            device_id=((me + step) % n_img, ori),
            device_id_type=MESH,
        )

    def code_arrival(step):
        other = (me + step) % n_img
        return pltpu.make_async_remote_copy(
            src_ref=codes,
            dst_ref=codes_buf.at[other],
            send_sem=code_send.at[step],
            recv_sem=code_recv.at[other],
            device_id=(other, ori),
            device_id_type=MESH,
        )

    def piece(src, sl, q, sems, to):
        return pltpu.make_async_remote_copy(
            src_ref=src,
            dst_ref=buf.at[sl, pl.ds(pl.multiple_of(q * quarter, quarter), quarter), :],
            send_sem=sems.at[sl * PARTS + q],
            recv_sem=recv_sem.at[sl * PARTS + q],
            device_id=(to, ori),
            device_id_type=MESH,
        )

    def held(sl, q):
        return buf.at[sl, pl.ds(pl.multiple_of(q * quarter, quarter), quarter), :]

    for h in range(PARTS):
        own = refs.at[pl.ds(h * quarter, quarter), :]

        @pl.when(has_up)
        def _():
            piece(own, me, h, up_sem, up).start()

        @pl.when(has_dn)
        def _():
            piece(own, me, h, dn_sem, dn).start()

        piece(own, me, h, y_sem, yn).start()

    own_copy.start()
    for f in range(n_img):
        image_copy(f).start()
    w_copy.start()
    for hop in range(nz - 1):
        greet(hop_sem.at[hop])
        pl.semaphore_wait(hop_sem.at[hop], near)
    for step in range(1, n_img):
        code_copy(step).start()

    codes_buf[me] = codes[...]
    sc[...] = jnp.zeros_like(sc)
    acc[...] = jnp.zeros_like(acc)
    own_copy.wait()
    for f in range(n_img):
        image_copy(f).wait()

    def brightest(i, top):
        f, at = i // (n_images // 16), pl.multiple_of((i % (n_images // 16)) * 16, 16)
        return jnp.maximum(top, jnp.abs(img_v[f, pl.ds(at, 16), :]))

    bright = lax.fori_loop(
        0, n_img * n_images // 16, brightest, jnp.zeros((16, depth), jnp.bfloat16)
    )
    bright = jnp.max(bright.astype(jnp.float32), axis=(0, 1), keepdims=True)

    def spread_codes():
        for step in range(1, n_img):
            code_arrival(step).wait_recv()
        low = lax.broadcasted_iota(jnp.int32, (th, LANES), 1) < per

        def unpacked(i):
            two = codes_buf[i]
            return jnp.concatenate([two % PACK, two // PACK], axis=0)

        for j in range(n_img // 2):
            a, b = unpacked(2 * j), unpacked(2 * j + 1)
            cut = slice(j * LANES, (j + 1) * LANES)
            codes_all[0:th, cut] = jnp.where(low, a, pltpu.roll(b, per, 1))
            codes_all[th:, cut] = jnp.where(low, pltpu.roll(a, per, 1), b)

    def place(s):
        r, q, k = s // (4 * PARTS), (s // 4) % PARTS, s % 4
        far = q >= PARTS // 2
        other = k // 2
        dist = r - other
        below = (k % 2) == 0
        slz = jnp.where(below, z - dist, z + dist)
        late = jnp.logical_and(jnp.logical_and(r == nz, far), k == 1)
        ok = jnp.logical_and(slz >= 0, slz < nz)
        ok = jnp.logical_and(ok, dist >= jnp.where(below, 0, 1))
        ok = jnp.logical_and(ok, dist < nz)
        skipped = jnp.logical_and(slz == zp, far)
        ok = jnp.logical_and(
            ok, jnp.logical_not(jnp.logical_and(other == 1, skipped))
        )
        ok = jnp.logical_or(ok, late)
        slz = jnp.where(late, zp, slz)
        sl = jnp.where(jnp.logical_or(other == 1, late), slz * NY + 1 - y, slz * NY + y)
        moving = jnp.logical_and(jnp.logical_and(other == 0, r > 0), jnp.logical_not(late))
        moving = jnp.logical_and(moving, ok)
        go_up = jnp.logical_and(jnp.logical_and(moving, below), has_up)
        go_dn = jnp.logical_and(jnp.logical_and(moving, jnp.logical_not(below)), has_dn)
        go_y = jnp.logical_and(moving, jnp.logical_not(skipped))
        sl = jnp.where(ok, sl, me)
        return r, q, k, sl, ok, go_up, go_dn, go_y

    steps = (nz + 1) * 4 * PARTS
    late_sl = z * NY + 1 - y

    strip = 16
    n_strips = half // strip
    factor = scale[...] * inv_root

    blocks = n_images // LANES

    def score_rows(at):
        return jnp.concatenate([sc[c, at, :] for c in range(blocks)], axis=1)

    def keep_rows(at, value):
        for c in range(blocks):
            sc[c, at, :] = value[:, c * LANES:(c + 1) * LANES]

    def half_softmax(h):
        def at_strip(i):
            i = h * n_strips + i
            flag = pattern[pl.ds(i // (group // strip), 1), :] > 0
            return pl.ds(pl.multiple_of(i * strip, strip), strip), flag

        def peak_of(i, m):
            at, flag = at_strip(i)
            s = jnp.where(flag, score_rows(at) * factor, -1e30)
            keep_rows(at, s)
            return jnp.maximum(m, s)

        m = lax.fori_loop(
            0, n_strips, peak_of, jnp.full((strip, n_images), -1e30, jnp.float32)
        )
        m = jnp.max(m, axis=0, keepdims=True)

        def mass_of(i, t):
            at, flag = at_strip(i)
            e = jnp.where(flag, jnp.exp(score_rows(at) - m), 0.0)
            keep_rows(at, e)
            return t + e

        t = lax.fori_loop(0, n_strips, mass_of, jnp.zeros((strip, n_images), jnp.float32))
        halves[2 * h:2 * h + 1, :] = m
        halves[2 * h + 1:2 * h + 2, :] = jnp.sum(t, axis=0, keepdims=True)

    first_hot = 2 * 4 * PARTS

    def arrive(s, carry):
        r, q, k, sl, ok, go_up, go_dn, go_y = place(s)

        @pl.when(s == (nz * PARTS + PARTS // 2) * 4)
        def _():
            half_softmax(0)

        @pl.when(s == first_hot)
        def _():
            spread_codes()

        @pl.when(jnp.logical_and(ok, r + k > 0))
        def _():
            piece(held(sl, q), sl, q, y_sem, yn).wait_recv()

        @pl.when(go_up)
        def _():
            piece(held(sl, q), sl, q, up_sem, up).start()

        @pl.when(go_dn)
        def _():
            piece(held(sl, q), sl, q, dn_sem, dn).start()

        @pl.when(go_y)
        def _():
            piece(held(sl, q), sl, q, y_sem, yn).start()

        turn = jnp.logical_and(r == nz - 1, jnp.logical_and(q == 0, k == 0))

        @pl.when(jnp.logical_and(turn, zp > z))
        def _():
            for late_q in range(PARTS // 2, PARTS):
                piece(held(late_sl, late_q), late_sl, late_q, up_sem, up).start()

        @pl.when(jnp.logical_and(turn, zp < z))
        def _():
            for late_q in range(PARTS // 2, PARTS):
                piece(held(late_sl, late_q), late_sl, late_q, dn_sem, dn).start()

        @pl.when(jnp.logical_and(ok, (q + 1) % (PARTS // 2) == 0))
        def _():
            at = pl.ds(pl.multiple_of((q // (PARTS // 2)) * half, half), half)
            term = lax.dot_general(
                buf[sl, at, :], img_v[sl], (((1,), (1,)), ((), ())),
                preferred_element_type=jnp.float32,
            )
            for c in range(blocks):
                sc[c, at, :] += term[:, c * LANES:(c + 1) * LANES]

        @pl.when(jnp.logical_and(s >= first_hot, s < first_hot + tiles_ref // 2))
        def _():
            for u in range(2):
                tile = 2 * (s - first_hot) + u
                code = codes_all[pl.ds(tile, 1), :]
                f, q = tile // chunk_tiles, tile % chunk_tiles
                at = pl.ds(pl.multiple_of(q * rows, rows), rows)

                def part(i, c):
                    base = pl.multiple_of(i * 64, 64)
                    row = lax.broadcasted_iota(jnp.int32, (64, rows), 0) + base
                    onehot[f, pl.ds(base, 64), at] = jnp.where(row == code, 1.0, 0.0).astype(
                        F8
                    )
                    return c

                lax.fori_loop(0, cells // 64, part, 0)

        return carry

    lax.fori_loop(0, steps, arrive, 0)

    half_softmax(1)
    m = jnp.maximum(halves[0:1, :], halves[2:3, :])
    total = halves[1:2, :] * jnp.exp(halves[0:1, :] - m)
    total += halves[3:4, :] * jnp.exp(halves[2:3, :] - m)
    stats[0:1, :] = m
    stats[1:2, :] = total

    def stat_copy(step, slot):
        return pltpu.make_async_remote_copy(
            src_ref=stats,
            dst_ref=stats_buf.at[slot],
            send_sem=stat_send.at[step],
            recv_sem=stat_recv.at[slot],
            device_id=(me, (ori + step) % n_ori),
            device_id_type=MESH,
        )

    for step in range(1, n_ori):
        stat_copy(step, ori).start()
    peak = m
    for step in range(1, n_ori):
        slot = (ori + step) % n_ori
        stat_copy(step, slot).wait_recv()
        peak = jnp.maximum(peak, stats_buf[slot, 0:1, :])
    mass = total * jnp.exp(m - peak)
    for step in range(1, n_ori):
        slot = (ori + step) % n_ori
        mass += stats_buf[slot, 1:2, :] * jnp.exp(stats_buf[slot, 0:1, :] - peak)
    stats_out[0:1, :] = peak
    stats_out[1:2, :] = mass
    share_of = scale[...] / mass

    spread = LANES // tiles_ref
    power = jnp.zeros((strip, LANES), jnp.float32)
    for h in range(2):
        weight = jnp.exp(halves[2 * h:2 * h + 1, :] - peak) * share_of

        def scale_of(i, top):
            i = h * n_strips + i
            first = (i // spread) * per + i % spread
            at = pl.ds(pl.multiple_of(i * strip, strip), strip)
            value = score_rows(pl.ds(first, strip, stride=spread)) * weight
            scaled[at, :] = value.astype(jnp.bfloat16)
            square = value * value
            held = square[:, 0:LANES]
            for c in range(1, blocks):
                held += square[:, c * LANES:(c + 1) * LANES]
            return jnp.maximum(top, held)

        power = lax.fori_loop(0, n_strips, scale_of, power)
    power = jnp.max(jnp.sum(power, axis=1, keepdims=True), axis=0, keepdims=True)
    largest = jnp.maximum(jnp.sqrt(power), 1e-15)
    largest = largest * (math.sqrt(n_images) * jnp.maximum(bright, 1e-18))
    grow, shrink = TOP / largest, largest * (1.0 / TOP)

    def values(f, j, rhs):
        value = jnp.dot(scaled[...], img_v[f], preferred_element_type=jnp.float32) * grow
        hi = value.astype(F8)
        lo = ((value - hi.astype(jnp.float32)) * LOW).astype(F8)
        for q in range(chunk_tiles):
            cut = slice(q * tile_width, (q + 1) * tile_width)
            rhs[j, q * rows:(q + 1) * rows, 0:tile_width] = hi[:, cut]
            rhs[j, q * rows:(q + 1) * rows, tile_width:] = lo[:, cut]

    x_me, core = ori // CORES, ori % CORES
    chips = n_ori // CORES
    side = cells // chips
    share = n_img * lines

    def collect(f, j, rhs, chip):
        at = pl.ds(pl.multiple_of(chip * side, side), side)
        acc[at, :] += jnp.dot(onehot[f, at, :], rhs[j], preferred_element_type=jnp.float32)

    def brick_terms(chip):
        at = pl.ds(pl.multiple_of(chip * side, side), side)
        both = acc[at, :]
        c = (both[:, 0:tile_width] + both[:, tile_width:] * (1.0 / LOW)) * shrink
        hi = c.astype(jnp.bfloat16)
        lo = (c - hi.astype(jnp.float32)).astype(jnp.bfloat16)
        n = side // positions
        wide_hi = jnp.concatenate([hi[p * n:(p + 1) * n, :] for p in range(positions)], axis=1)
        wide_lo = jnp.concatenate([lo[p * n:(p + 1) * n, :] for p in range(positions)], axis=1)
        brick = jnp.dot(wide_hi, w_v[...], preferred_element_type=jnp.float32)
        brick += jnp.dot(wide_lo, w_v[...], preferred_element_type=jnp.float32)
        for c in range(CORES):
            terms[chip * CORES + c] = brick[c * share:(c + 1) * share, :]

    def term_copy(to, slot):
        return pltpu.make_async_remote_copy(
            src_ref=terms.at[to],
            dst_ref=terms_buf.at[slot],
            send_sem=a_send.at[to],
            recv_sem=a_recv.at[slot],
            device_id=(me, to),
            device_id_type=MESH,
        )

    values(0, 0, rhs_a)

    def first_side(j, c):
        values(2 * j + 1, j, rhs_b)
        collect(2 * j, j, rhs_a, 1 - x_me)
        values(2 * j + 2, j + 1, rhs_a)
        collect(2 * j + 1, j, rhs_b, 1 - x_me)
        return c

    last = n_img // 2 - 1
    lax.fori_loop(0, last, first_side, 0)
    values(n_img - 1, last, rhs_b)
    collect(n_img - 2, last, rhs_a, 1 - x_me)
    collect(n_img - 1, last, rhs_b, 1 - x_me)
    w_copy.wait()
    brick_terms(1 - x_me)
    for c in range(CORES):
        term_copy((1 - x_me) * CORES + c, ori).start()

    def second_side(j, c):
        collect(2 * j, j, rhs_a, x_me)
        collect(2 * j + 1, j, rhs_b, x_me)
        return c

    lax.fori_loop(0, n_img // 2, second_side, 0)
    brick_terms(x_me)
    mate = x_me * CORES + 1 - core
    term_copy(mate, ori).start()
    mine = terms[ori]
    term_copy(mate, mate).wait_recv()
    mine += terms_buf[mate]
    for c in range(CORES):
        slot = (1 - x_me) * CORES + c
        term_copy(slot, slot).wait_recv()
        mine += terms_buf[slot]
    for i in range(n_img):
        mid[i] = mine[i * lines:(i + 1) * lines, :]

    def mid_copy(step, slot):
        to = (me + step) % n_img
        return pltpu.make_async_remote_copy(
            src_ref=mid.at[to],
            dst_ref=mid_buf.at[slot],
            send_sem=b_send.at[step],
            recv_sem=b_recv.at[slot],
            device_id=(to, ori),
            device_id_type=MESH,
        )

    for step in range(1, n_img):
        mid_copy(step, me).start()
    for step in range(1, n_img):
        code_copy(step).wait_send()
    for step in range(1, n_ori):
        stat_copy(step, ori).wait_send()
        term_copy((ori + step) % n_ori, ori).wait_send()
    for h in range(PARTS):
        own = refs.at[pl.ds(h * quarter, quarter), :]

        @pl.when(has_up)
        def _():
            piece(own, me, h, up_sem, up).wait_send()

        @pl.when(has_dn)
        def _():
            piece(own, me, h, dn_sem, dn).wait_send()

        piece(own, me, h, y_sem, yn).wait_send()

    @pl.when(zp > z)
    def _():
        for late_q in range(PARTS // 2, PARTS):
            piece(held(late_sl, late_q), late_sl, late_q, up_sem, up).wait_send()

    @pl.when(zp < z)
    def _():
        for late_q in range(PARTS // 2, PARTS):
            piece(held(late_sl, late_q), late_sl, late_q, dn_sem, dn).wait_send()

    def drain(s, carry):
        r, q, k, sl, ok, go_up, go_dn, go_y = place(s)

        @pl.when(go_up)
        def _():
            piece(held(sl, q), sl, q, up_sem, up).wait_send()

        @pl.when(go_dn)
        def _():
            piece(held(sl, q), sl, q, dn_sem, dn).wait_send()

        @pl.when(go_y)
        def _():
            piece(held(sl, q), sl, q, y_sem, yn).wait_send()

        return carry

    lax.fori_loop(0, steps, drain, 0)

    result = mid[me]
    for step in range(1, n_img):
        slot = (me + step) % n_img
        mid_copy(step, slot).wait_recv()
        if step < n_img - 1:
            result += mid_buf[slot]
    sums_out[0] = result
    sums_out[1] = mid_buf[(me + n_img - 1) % n_img]
    for step in range(1, n_img):
        mid_copy(step, me).wait_send()


def finish(sums, stats, bricks, evidence):
    bricks[...] = sums[0] + sums[1]
    evidence[...] = stats[0:1, :] + jnp.log(stats[1:2, :])


def fused_body(
    images, img_scale, references, pattern, tile_owner, tile_brick, tile_block, distance_weights
):
    n_img, n_ori = lax.axis_size("img"), lax.axis_size("ori")
    n_images, width = images.shape
    rows, depth = references.shape
    positions, tile_width, voxels = distance_weights.shape
    tiles_ref = width // tile_width
    lines = BRICK_DEV // n_ori
    cells = n_img * BRICK_DEV * positions
    flat = (tile_brick.size // LANES, LANES)
    bf16, f32, i32 = jnp.bfloat16, jnp.float32, jnp.int32
    vmem = pl.BlockSpec(memory_space=pltpu.VMEM)
    hbm = pl.BlockSpec(memory_space=pl.ANY)
    dma = pltpu.SemaphoreType.DMA
    sums, stats = pl.pallas_call(
        functools.partial(kernel, n_img, n_ori, tiles_ref, 1.0 / math.sqrt(width)),
        out_shape=(
            jax.ShapeDtypeStruct((2, lines, voxels), f32),
            jax.ShapeDtypeStruct((2, n_images), f32),
        ),
        in_specs=[hbm, hbm, vmem, vmem, vmem, vmem, vmem, hbm],
        out_specs=(vmem, vmem),
        scratch_shapes=[
            pltpu.VMEM((n_img, n_images, depth), bf16),
            pltpu.VMEM((n_img, rows, depth), bf16),
            pltpu.VMEM((positions * tile_width, voxels), bf16),
            pltpu.VMEM((n_images // LANES, rows, LANES), f32),
            pltpu.VMEM((rows, n_images), bf16),
            pltpu.VMEM((tiles_ref // 4, LANES), i32),
            pltpu.VMEM((n_img, tiles_ref // 4, LANES), i32),
            pltpu.VMEM((tiles_ref, rows), i32),
            pltpu.VMEM((n_img, cells, rows * depth // tile_width), F8),
            pltpu.VMEM((n_img // 2, rows * depth // tile_width, 2 * tile_width), F8),
            pltpu.VMEM((n_img // 2, rows * depth // tile_width, 2 * tile_width), F8),
            pltpu.VMEM((cells, 2 * tile_width), f32),
            pltpu.VMEM((4, n_images), f32),
            pltpu.VMEM((2, n_images), f32),
            pltpu.VMEM((n_ori, 2, n_images), f32),
            pltpu.VMEM((n_ori, n_img * lines, voxels), f32),
            pltpu.VMEM((n_ori, n_img * lines, voxels), f32),
            pltpu.VMEM((n_img, lines, voxels), f32),
            pltpu.VMEM((n_img, lines, voxels), f32),
            dma((n_img,)),
            dma,
            dma,
            dma((PARTS * n_img,)),
            dma((PARTS * n_img,)),
            dma((PARTS * n_img,)),
            dma((PARTS * n_img,)),
            dma((n_img,)),
            dma((n_img,)),
            dma((n_ori,)),
            dma((n_ori,)),
            dma((n_ori,)),
            dma((n_ori,)),
            dma((n_img,)),
            dma((n_img,)),
            pltpu.SemaphoreType.REGULAR((n_img // NY - 1,)),
        ],
        compiler_params=pltpu.CompilerParams(
            collective_id=0, has_side_effects=True, vmem_limit_bytes=67043328
        ),
    )(
        references,
        images,
        img_scale[None, :],
        pattern.T,
        tile_owner.reshape(flat),
        tile_brick.reshape(flat),
        tile_block.reshape(flat),
        distance_weights.reshape(positions * tile_width, voxels),
    )
    bricks, evidence = pl.pallas_call(
        finish,
        out_shape=(
            jax.ShapeDtypeStruct((lines, voxels), f32),
            jax.ShapeDtypeStruct((1, n_images), f32),
        ),
        in_specs=[vmem, vmem],
        out_specs=(vmem, vmem),
    )(sums, stats)
    return bricks, evidence.reshape(-1)


def body(*args):
    images, references, weights = args[0], args[2], args[7]
    n_img = lax.axis_size("img")
    rows, depth = references.shape
    cells = n_img * BRICK_DEV * weights.shape[0]
    tiles_ref = images.shape[1] // weights.shape[1]
    room = 2 * (images.size + rows * depth * n_img * (1 + cells // weights.shape[1]))
    fits = (
        depth % LANES == 0
        and 2 * (rows // n_img) == LANES
        and LANES % tiles_ref == 0
        and tiles_ref % 32 == 0
        and cells <= PACK // 2
        and lax.axis_size("ori") == 2 * CORES
        and rows * tiles_ref == 16 * LANES * n_img
        and n_img % (2 * NY) == 0
        and n_img >= 4 * NY
        and room < 48 * 2**20
    )
    return fused_body(*args) if fits else plain_body(*args)


def solution(mesh):
    placed = (
        P("img", None),
        P("img"),
        P("ori", "img"),
        P("img", "ori"),
        P("ori", "img", None),
        P("ori", "img"),
        P("ori", "img"),
        P(),
    )
    return jax.shard_map(
        body,
        mesh=mesh,
        in_specs=placed,
        out_specs=(P(("img", "ori"), None), P("img")),
        check_vma=False,
    )
```

```python
import functools
import math

import jax
import jax.numpy as jnp
from jax import lax
from jax.experimental import pallas as pl
from jax.experimental.pallas import tpu as pltpu
from jax.sharding import PartitionSpec as P

BRICK_DEV = 16
LANES = 128
NY = 2
PARTS = 2
CORES = 2
PACK = 1 << 16
F8 = jnp.float8_e4m3fn
TOP = 256.0
LOW = 32.0
MESH = pl.DeviceIdType.MESH


def plain_body(
    images, img_scale, references, pattern, tile_owner, tile_brick, tile_block, distance_weights
):
    image_rows, width = images.shape
    ref_local = references.shape[0]
    group_size = ref_local // pattern.shape[1]
    positions, tile_width, voxels = distance_weights.shape
    inv_root = 1.0 / math.sqrt(width)
    weight_table = distance_weights.astype(jnp.float32)
    raw_scores = lax.dot_general(
        images,
        lax.all_gather(references, "img", axis=1, tiled=True),
        (((1,), (1,)), ((), ())),
        preferred_element_type=jnp.float32,
    )
    scores = raw_scores * img_scale[:, None] * inv_root
    active = jnp.repeat(pattern > 0, group_size, axis=1)
    masked = jnp.where(active, scores, -1e30)
    local_peak = jnp.max(masked, axis=1)
    peak = lax.pmax(local_peak, "ori")
    expo = jnp.where(active, jnp.exp(masked - peak[:, None]), 0.0)
    mass = lax.psum(jnp.sum(expo, axis=1), "ori")
    weights = expo / mass[:, None]
    log_evidence = peak + jnp.log(mass)
    scaled = (weights * img_scale[:, None]).astype(jnp.bfloat16)
    partial_value = lax.dot_general(
        scaled, images, (((0,), (0,)), ((), ())), preferred_element_type=jnp.float32
    )
    owners = tile_owner.reshape(-1)
    local_code = tile_brick.reshape(-1) * positions + tile_block.reshape(-1)
    cells = BRICK_DEV * positions
    tile_code = owners * cells + local_code
    group_code = lax.all_gather(tile_code, "img", axis=0, tiled=True)
    peers = lax.axis_size("img")
    group_tiles = partial_value.reshape(-1, tile_width)
    collected = jax.ops.segment_sum(group_tiles, group_code, num_segments=peers * cells)
    brick_terms = jnp.einsum(
        "bpt,ptv->bv",
        collected.reshape(peers * BRICK_DEV, positions, tile_width),
        weight_table,
        precision=lax.Precision.HIGHEST,
    )
    bricks = lax.psum_scatter(brick_terms, ("img", "ori"), scatter_dimension=0, tiled=True)
    return (bricks, log_evidence)


def kernel(
    n_img, n_ori, tiles_ref, inv_root,
    refs, images, scale, pattern, owner, brick_of, block_of, weights,
    sums_out, stats_out,
    img_v, buf, w_v, sc, scaled, codes, codes_buf, codes_all, onehot, rhs_a, rhs_b, acc,
    halves, stats, stats_buf, terms, terms_buf, mid, mid_buf,
    img_sem, w_sem, own_sem, up_sem, dn_sem, y_sem, recv_sem, code_send, code_recv,
    stat_send, stat_recv, a_send, a_recv, b_send, b_recv, hop_sem,
):
    nz = n_img // NY
    me = lax.axis_index("img")
    ori = lax.axis_index("ori")
    z, y = me // NY, me % NY
    zp = z + 1 - 2 * (z % 2)
    rows, depth = refs.shape
    half = rows // 2
    quarter = rows // PARTS
    n_images = img_v.shape[1]
    groups = pattern.shape[0]
    group = rows // groups
    tile_width, (depth_w, voxels) = acc.shape[1] // 2, w_v.shape
    positions = depth_w // tile_width
    chunk_tiles = depth // tile_width
    cells = acc.shape[0]

    def image_copy(f):
        return pltpu.make_async_copy(
            images.at[:, pl.ds(f * depth, depth)], img_v.at[f], img_sem.at[f]
        )

    w_copy = pltpu.make_async_copy(weights, w_v, w_sem)
    own_copy = pltpu.make_async_copy(refs, buf.at[me], own_sem)

    up, dn, yn = me + NY, me - NY, z * NY + 1 - y
    has_up, has_dn = z < nz - 1, z > 0
    near = 1 + has_up.astype(jnp.int32) + has_dn.astype(jnp.int32)

    def greet(sem):
        @pl.when(has_up)
        def _():
            pl.semaphore_signal(sem, inc=1, device_id=(up, ori), device_id_type=MESH)

        @pl.when(has_dn)
        def _():
            pl.semaphore_signal(sem, inc=1, device_id=(dn, ori), device_id_type=MESH)

        pl.semaphore_signal(sem, inc=1, device_id=(yn, ori), device_id_type=MESH)

    barrier = pltpu.get_barrier_semaphore()
    greet(barrier)
    for step in range(1, n_ori):
        pl.semaphore_signal(
            barrier, inc=1, device_id=(me, (ori + step) % n_ori), device_id_type=MESH
        )
    per = rows // n_img
    th = tiles_ref // 2
    lines = BRICK_DEV // n_ori
    brick_ids = brick_of[...]
    place_of = brick_ids // lines
    raw = (
        (place_of // CORES) * (cells // (n_ori // CORES))
        + block_of[...] * (CORES * n_img * lines)
        + (place_of % CORES) * (n_img * lines)
        + owner[...] * lines
        + brick_ids % lines
    )
    held_rows = raw.shape[0]
    turned = jnp.concatenate(
        [raw, jnp.zeros((LANES - held_rows, LANES), jnp.int32)], axis=0
    ).T
    local = jnp.zeros((tiles_ref, LANES), jnp.int32)
    for j in range(LANES // tiles_ref):
        cut = turned[j * tiles_ref:(j + 1) * tiles_ref, :]
        local += pltpu.roll(cut, j * held_rows, 1) if j else cut
    wide = local[0:th, :] + pltpu.roll(local[th:, :], per, 1)
    codes[...] = wide[0:th // 2, :] + wide[th // 2:, :] * PACK

    pl.semaphore_wait(barrier, near + n_ori - 1)

    def code_copy(step):
        return pltpu.make_async_remote_copy(
            src_ref=codes,
            dst_ref=codes_buf.at[me],
            send_sem=code_send.at[step],
            recv_sem=code_recv.at[me],
            device_id=((me + step) % n_img, ori),
            device_id_type=MESH,
        )

    def code_arrival(step):
        other = (me + step) % n_img
        return pltpu.make_async_remote_copy(
            src_ref=codes,
            dst_ref=codes_buf.at[other],
            send_sem=code_send.at[step],
            recv_sem=code_recv.at[other],
            device_id=(other, ori),
            device_id_type=MESH,
        )

    def piece(src, sl, q, sems, to):
        return pltpu.make_async_remote_copy(
            src_ref=src,
            dst_ref=buf.at[sl, pl.ds(pl.multiple_of(q * quarter, quarter), quarter), :],
            send_sem=sems.at[sl * PARTS + q],
            recv_sem=recv_sem.at[sl * PARTS + q],
            device_id=(to, ori),
            device_id_type=MESH,
        )

    def held(sl, q):
        return buf.at[sl, pl.ds(pl.multiple_of(q * quarter, quarter), quarter), :]

    for h in range(PARTS):
        own = refs.at[pl.ds(h * quarter, quarter), :]

        @pl.when(has_up)
        def _():
            piece(own, me, h, up_sem, up).start()

        @pl.when(has_dn)
        def _():
            piece(own, me, h, dn_sem, dn).start()

        piece(own, me, h, y_sem, yn).start()

    own_copy.start()
    for f in range(n_img):
        image_copy(f).start()
    w_copy.start()
    for hop in range(nz - 1):
        greet(hop_sem.at[hop])
        pl.semaphore_wait(hop_sem.at[hop], near)
    for step in range(1, n_img):
        code_copy(step).start()

    codes_buf[me] = codes[...]
    sc[...] = jnp.zeros_like(sc)
    acc[...] = jnp.zeros_like(acc)
    own_copy.wait()
    for f in range(n_img):
        image_copy(f).wait()

    def brightest(i, top):
        f, at = i // (n_images // 16), pl.multiple_of((i % (n_images // 16)) * 16, 16)
        return jnp.maximum(top, jnp.abs(img_v[f, pl.ds(at, 16), :]))

    bright = lax.fori_loop(
        0, n_img * n_images // 16, brightest, jnp.zeros((16, depth), jnp.bfloat16)
    )
    bright = jnp.max(bright.astype(jnp.float32), axis=(0, 1), keepdims=True)

    def spread_codes():
        for step in range(1, n_img):
            code_arrival(step).wait_recv()
        low = lax.broadcasted_iota(jnp.int32, (th, LANES), 1) < per

        def unpacked(i):
            two = codes_buf[i]
            return jnp.concatenate([two % PACK, two // PACK], axis=0)

        for j in range(n_img // 2):
            a, b = unpacked(2 * j), unpacked(2 * j + 1)
            cut = slice(j * LANES, (j + 1) * LANES)
            codes_all[0:th, cut] = jnp.where(low, a, pltpu.roll(b, per, 1))
            codes_all[th:, cut] = jnp.where(low, pltpu.roll(a, per, 1), b)

    def place(s):
        r, q, k = s // (4 * PARTS), (s // 4) % PARTS, s % 4
        far = q >= PARTS // 2
        other = k // 2
        dist = r - other
        below = (k % 2) == 0
        slz = jnp.where(below, z - dist, z + dist)
        late = jnp.logical_and(jnp.logical_and(r == nz, far), k == 1)
        ok = jnp.logical_and(slz >= 0, slz < nz)
        ok = jnp.logical_and(ok, dist >= jnp.where(below, 0, 1))
        ok = jnp.logical_and(ok, dist < nz)
        skipped = jnp.logical_and(slz == zp, far)
        ok = jnp.logical_and(
            ok, jnp.logical_not(jnp.logical_and(other == 1, skipped))
        )
        ok = jnp.logical_or(ok, late)
        slz = jnp.where(late, zp, slz)
        sl = jnp.where(jnp.logical_or(other == 1, late), slz * NY + 1 - y, slz * NY + y)
        moving = jnp.logical_and(jnp.logical_and(other == 0, r > 0), jnp.logical_not(late))
        moving = jnp.logical_and(moving, ok)
        go_up = jnp.logical_and(jnp.logical_and(moving, below), has_up)
        go_dn = jnp.logical_and(jnp.logical_and(moving, jnp.logical_not(below)), has_dn)
        go_y = jnp.logical_and(moving, jnp.logical_not(skipped))
        sl = jnp.where(ok, sl, me)
        return r, q, k, sl, ok, go_up, go_dn, go_y

    steps = (nz + 1) * 4 * PARTS
    late_sl = z * NY + 1 - y

    strip = 16
    n_strips = half // strip
    factor = scale[...] * inv_root

    blocks = n_images // LANES

    def score_rows(at):
        return jnp.concatenate([sc[c, at, :] for c in range(blocks)], axis=1)

    def keep_rows(at, value):
        for c in range(blocks):
            sc[c, at, :] = value[:, c * LANES:(c + 1) * LANES]

    def half_softmax(h):
        def at_strip(i):
            i = h * n_strips + i
            flag = pattern[pl.ds(i // (group // strip), 1), :] > 0
            return pl.ds(pl.multiple_of(i * strip, strip), strip), flag

        def peak_of(i, m):
            at, flag = at_strip(i)
            s = jnp.where(flag, score_rows(at) * factor, -1e30)
            keep_rows(at, s)
            return jnp.maximum(m, s)

        m = lax.fori_loop(
            0, n_strips, peak_of, jnp.full((strip, n_images), -1e30, jnp.float32)
        )
        m = jnp.max(m, axis=0, keepdims=True)

        def mass_of(i, t):
            at, flag = at_strip(i)
            e = jnp.where(flag, jnp.exp(score_rows(at) - m), 0.0)
            keep_rows(at, e)
            return t + e

        t = lax.fori_loop(0, n_strips, mass_of, jnp.zeros((strip, n_images), jnp.float32))
        halves[2 * h:2 * h + 1, :] = m
        halves[2 * h + 1:2 * h + 2, :] = jnp.sum(t, axis=0, keepdims=True)

    first_hot = 2 * 4 * PARTS

    def arrive(s, carry):
        r, q, k, sl, ok, go_up, go_dn, go_y = place(s)

        @pl.when(s == (nz * PARTS + PARTS // 2) * 4)
        def _():
            half_softmax(0)

        @pl.when(s == first_hot)
        def _():
            spread_codes()

        @pl.when(jnp.logical_and(ok, r + k > 0))
        def _():
            piece(held(sl, q), sl, q, y_sem, yn).wait_recv()

        @pl.when(go_up)
        def _():
            piece(held(sl, q), sl, q, up_sem, up).start()

        @pl.when(go_dn)
        def _():
            piece(held(sl, q), sl, q, dn_sem, dn).start()

        @pl.when(go_y)
        def _():
            piece(held(sl, q), sl, q, y_sem, yn).start()

        turn = jnp.logical_and(r == nz - 1, jnp.logical_and(q == 0, k == 0))

        @pl.when(jnp.logical_and(turn, zp > z))
        def _():
            for late_q in range(PARTS // 2, PARTS):
                piece(held(late_sl, late_q), late_sl, late_q, up_sem, up).start()

        @pl.when(jnp.logical_and(turn, zp < z))
        def _():
            for late_q in range(PARTS // 2, PARTS):
                piece(held(late_sl, late_q), late_sl, late_q, dn_sem, dn).start()

        @pl.when(jnp.logical_and(ok, (q + 1) % (PARTS // 2) == 0))
        def _():
            at = pl.ds(pl.multiple_of((q // (PARTS // 2)) * half, half), half)
            term = lax.dot_general(
                buf[sl, at, :], img_v[sl], (((1,), (1,)), ((), ())),
                preferred_element_type=jnp.float32,
            )
            for c in range(blocks):
                sc[c, at, :] += term[:, c * LANES:(c + 1) * LANES]

        @pl.when(jnp.logical_and(s >= first_hot, s < first_hot + tiles_ref // 2))
        def _():
            for u in range(2):
                tile = 2 * (s - first_hot) + u
                code = codes_all[pl.ds(tile, 1), :]
                f, q = tile // chunk_tiles, tile % chunk_tiles
                at = pl.ds(pl.multiple_of(q * rows, rows), rows)

                def part(i, c):
                    base = pl.multiple_of(i * 64, 64)
                    row = lax.broadcasted_iota(jnp.int32, (64, rows), 0) + base
                    onehot[f, pl.ds(base, 64), at] = jnp.where(row == code, 1.0, 0.0).astype(
                        F8
                    )
                    return c

                lax.fori_loop(0, cells // 64, part, 0)

        return carry

    lax.fori_loop(0, steps, arrive, 0)

    half_softmax(1)
    m = jnp.maximum(halves[0:1, :], halves[2:3, :])
    total = halves[1:2, :] * jnp.exp(halves[0:1, :] - m)
    total += halves[3:4, :] * jnp.exp(halves[2:3, :] - m)
    stats[0:1, :] = m
    stats[1:2, :] = total

    def stat_copy(step, slot):
        return pltpu.make_async_remote_copy(
            src_ref=stats,
            dst_ref=stats_buf.at[slot],
            send_sem=stat_send.at[step],
            recv_sem=stat_recv.at[slot],
            device_id=(me, (ori + step) % n_ori),
            device_id_type=MESH,
        )

    for step in range(1, n_ori):
        stat_copy(step, ori).start()
    peak = m
    for step in range(1, n_ori):
        slot = (ori + step) % n_ori
        stat_copy(step, slot).wait_recv()
        peak = jnp.maximum(peak, stats_buf[slot, 0:1, :])
    mass = total * jnp.exp(m - peak)
    for step in range(1, n_ori):
        slot = (ori + step) % n_ori
        mass += stats_buf[slot, 1:2, :] * jnp.exp(stats_buf[slot, 0:1, :] - peak)
    stats_out[0:1, :] = peak
    stats_out[1:2, :] = mass
    share_of = scale[...] / mass

    spread = LANES // tiles_ref
    power = jnp.zeros((strip, LANES), jnp.float32)
    for h in range(2):
        weight = jnp.exp(halves[2 * h:2 * h + 1, :] - peak) * share_of

        def scale_of(i, top):
            i = h * n_strips + i
            first = (i // spread) * per + i % spread
            at = pl.ds(pl.multiple_of(i * strip, strip), strip)
            value = score_rows(pl.ds(first, strip, stride=spread)) * weight
            scaled[at, :] = value.astype(jnp.bfloat16)
            square = value * value
            held = square[:, 0:LANES]
            for c in range(1, blocks):
                held += square[:, c * LANES:(c + 1) * LANES]
            return jnp.maximum(top, held)

        power = lax.fori_loop(0, n_strips, scale_of, power)
    power = jnp.max(jnp.sum(power, axis=1, keepdims=True), axis=0, keepdims=True)
    largest = jnp.maximum(jnp.sqrt(power), 1e-15)
    largest = largest * (math.sqrt(n_images) * jnp.maximum(bright, 1e-18))
    grow, shrink = TOP / largest, largest * (1.0 / TOP)

    def values(f, j, rhs):
        value = jnp.dot(scaled[...], img_v[f], preferred_element_type=jnp.float32) * grow
        hi = value.astype(F8)
        lo = ((value - hi.astype(jnp.float32)) * LOW).astype(F8)
        for q in range(chunk_tiles):
            cut = slice(q * tile_width, (q + 1) * tile_width)
            rhs[j, q * rows:(q + 1) * rows, 0:tile_width] = hi[:, cut]
            rhs[j, q * rows:(q + 1) * rows, tile_width:] = lo[:, cut]

    x_me, core = ori // CORES, ori % CORES
    chips = n_ori // CORES
    side = cells // chips
    share = n_img * lines

    def collect(f, j, rhs, chip):
        at = pl.ds(pl.multiple_of(chip * side, side), side)
        acc[at, :] += jnp.dot(onehot[f, at, :], rhs[j], preferred_element_type=jnp.float32)

    def brick_terms(chip):
        at = pl.ds(pl.multiple_of(chip * side, side), side)
        both = acc[at, :]
        c = (both[:, 0:tile_width] + both[:, tile_width:] * (1.0 / LOW)) * shrink
        hi = c.astype(jnp.bfloat16)
        lo = (c - hi.astype(jnp.float32)).astype(jnp.bfloat16)
        n = side // positions
        wide_hi = jnp.concatenate([hi[p * n:(p + 1) * n, :] for p in range(positions)], axis=1)
        wide_lo = jnp.concatenate([lo[p * n:(p + 1) * n, :] for p in range(positions)], axis=1)
        wide = jnp.concatenate([wide_hi, wide_lo], axis=0)
        brick = jnp.dot(wide, w_v[...], preferred_element_type=jnp.float32)
        brick = brick[0:n, :] + brick[n:, :]
        for c in range(CORES):
            terms[chip * CORES + c] = brick[c * share:(c + 1) * share, :]

    def term_copy(to, slot):
        return pltpu.make_async_remote_copy(
            src_ref=terms.at[to],
            dst_ref=terms_buf.at[slot],
            send_sem=a_send.at[to],
            recv_sem=a_recv.at[slot],
            device_id=(me, to),
            device_id_type=MESH,
        )

    values(0, 0, rhs_a)

    def first_side(j, c):
        values(2 * j + 1, j, rhs_b)
        collect(2 * j, j, rhs_a, 1 - x_me)
        values(2 * j + 2, j + 1, rhs_a)
        collect(2 * j + 1, j, rhs_b, 1 - x_me)
        return c

    last = n_img // 2 - 1
    lax.fori_loop(0, last, first_side, 0)
    values(n_img - 1, last, rhs_b)
    collect(n_img - 2, last, rhs_a, 1 - x_me)
    collect(n_img - 1, last, rhs_b, 1 - x_me)
    w_copy.wait()
    brick_terms(1 - x_me)
    for c in range(CORES):
        term_copy((1 - x_me) * CORES + c, ori).start()

    def second_side(j, c):
        collect(2 * j, j, rhs_a, x_me)
        collect(2 * j + 1, j, rhs_b, x_me)
        return c

    lax.fori_loop(0, n_img // 2, second_side, 0)
    brick_terms(x_me)
    mate = x_me * CORES + 1 - core
    term_copy(mate, ori).start()
    mine = terms[ori]
    term_copy(mate, mate).wait_recv()
    mine += terms_buf[mate]
    for c in range(CORES):
        slot = (1 - x_me) * CORES + c
        term_copy(slot, slot).wait_recv()
        mine += terms_buf[slot]
    for i in range(n_img):
        mid[i] = mine[i * lines:(i + 1) * lines, :]

    def mid_copy(step, slot):
        to = (me + step) % n_img
        return pltpu.make_async_remote_copy(
            src_ref=mid.at[to],
            dst_ref=mid_buf.at[slot],
            send_sem=b_send.at[step],
            recv_sem=b_recv.at[slot],
            device_id=(to, ori),
            device_id_type=MESH,
        )

    for step in range(1, n_img):
        mid_copy(step, me).start()
    for step in range(1, n_img):
        code_copy(step).wait_send()
    for step in range(1, n_ori):
        stat_copy(step, ori).wait_send()
        term_copy((ori + step) % n_ori, ori).wait_send()
    for h in range(PARTS):
        own = refs.at[pl.ds(h * quarter, quarter), :]

        @pl.when(has_up)
        def _():
            piece(own, me, h, up_sem, up).wait_send()

        @pl.when(has_dn)
        def _():
            piece(own, me, h, dn_sem, dn).wait_send()

        piece(own, me, h, y_sem, yn).wait_send()

    @pl.when(zp > z)
    def _():
        for late_q in range(PARTS // 2, PARTS):
            piece(held(late_sl, late_q), late_sl, late_q, up_sem, up).wait_send()

    @pl.when(zp < z)
    def _():
        for late_q in range(PARTS // 2, PARTS):
            piece(held(late_sl, late_q), late_sl, late_q, dn_sem, dn).wait_send()

    def drain(s, carry):
        r, q, k, sl, ok, go_up, go_dn, go_y = place(s)

        @pl.when(go_up)
        def _():
            piece(held(sl, q), sl, q, up_sem, up).wait_send()

        @pl.when(go_dn)
        def _():
            piece(held(sl, q), sl, q, dn_sem, dn).wait_send()

        @pl.when(go_y)
        def _():
            piece(held(sl, q), sl, q, y_sem, yn).wait_send()

        return carry

    lax.fori_loop(0, steps, drain, 0)

    result = mid[me]
    for step in range(1, n_img):
        slot = (me + step) % n_img
        mid_copy(step, slot).wait_recv()
        if step < n_img - 1:
            result += mid_buf[slot]
    sums_out[0] = result
    sums_out[1] = mid_buf[(me + n_img - 1) % n_img]
    for step in range(1, n_img):
        mid_copy(step, me).wait_send()


def finish(sums, stats, bricks, evidence):
    bricks[...] = sums[0] + sums[1]
    evidence[...] = stats[0:1, :] + jnp.log(stats[1:2, :])


def fused_body(
    images, img_scale, references, pattern, tile_owner, tile_brick, tile_block, distance_weights
):
    n_img, n_ori = lax.axis_size("img"), lax.axis_size("ori")
    n_images, width = images.shape
    rows, depth = references.shape
    positions, tile_width, voxels = distance_weights.shape
    tiles_ref = width // tile_width
    lines = BRICK_DEV // n_ori
    cells = n_img * BRICK_DEV * positions
    flat = (tile_brick.size // LANES, LANES)
    bf16, f32, i32 = jnp.bfloat16, jnp.float32, jnp.int32
    vmem = pl.BlockSpec(memory_space=pltpu.VMEM)
    hbm = pl.BlockSpec(memory_space=pl.ANY)
    dma = pltpu.SemaphoreType.DMA
    sums, stats = pl.pallas_call(
        functools.partial(kernel, n_img, n_ori, tiles_ref, 1.0 / math.sqrt(width)),
        out_shape=(
            jax.ShapeDtypeStruct((2, lines, voxels), f32),
            jax.ShapeDtypeStruct((2, n_images), f32),
        ),
        in_specs=[hbm, hbm, vmem, vmem, vmem, vmem, vmem, hbm],
        out_specs=(vmem, vmem),
        scratch_shapes=[
            pltpu.VMEM((n_img, n_images, depth), bf16),
            pltpu.VMEM((n_img, rows, depth), bf16),
            pltpu.VMEM((positions * tile_width, voxels), bf16),
            pltpu.VMEM((n_images // LANES, rows, LANES), f32),
            pltpu.VMEM((rows, n_images), bf16),
            pltpu.VMEM((tiles_ref // 4, LANES), i32),
            pltpu.VMEM((n_img, tiles_ref // 4, LANES), i32),
            pltpu.VMEM((tiles_ref, rows), i32),
            pltpu.VMEM((n_img, cells, rows * depth // tile_width), F8),
            pltpu.VMEM((n_img // 2, rows * depth // tile_width, 2 * tile_width), F8),
            pltpu.VMEM((n_img // 2, rows * depth // tile_width, 2 * tile_width), F8),
            pltpu.VMEM((cells, 2 * tile_width), f32),
            pltpu.VMEM((4, n_images), f32),
            pltpu.VMEM((2, n_images), f32),
            pltpu.VMEM((n_ori, 2, n_images), f32),
            pltpu.VMEM((n_ori, n_img * lines, voxels), f32),
            pltpu.VMEM((n_ori, n_img * lines, voxels), f32),
            pltpu.VMEM((n_img, lines, voxels), f32),
            pltpu.VMEM((n_img, lines, voxels), f32),
            dma((n_img,)),
            dma,
            dma,
            dma((PARTS * n_img,)),
            dma((PARTS * n_img,)),
            dma((PARTS * n_img,)),
            dma((PARTS * n_img,)),
            dma((n_img,)),
            dma((n_img,)),
            dma((n_ori,)),
            dma((n_ori,)),
            dma((n_ori,)),
            dma((n_ori,)),
            dma((n_img,)),
            dma((n_img,)),
            pltpu.SemaphoreType.REGULAR((n_img // NY - 1,)),
        ],
        compiler_params=pltpu.CompilerParams(
            collective_id=0, has_side_effects=True, vmem_limit_bytes=67043328
        ),
    )(
        references,
        images,
        img_scale[None, :],
        pattern.T,
        tile_owner.reshape(flat),
        tile_brick.reshape(flat),
        tile_block.reshape(flat),
        distance_weights.reshape(positions * tile_width, voxels),
    )
    bricks, evidence = pl.pallas_call(
        finish,
        out_shape=(
            jax.ShapeDtypeStruct((lines, voxels), f32),
            jax.ShapeDtypeStruct((1, n_images), f32),
        ),
        in_specs=[vmem, vmem],
        out_specs=(vmem, vmem),
    )(sums, stats)
    return bricks, evidence.reshape(-1)


def body(*args):
    images, references, weights = args[0], args[2], args[7]
    n_img = lax.axis_size("img")
    rows, depth = references.shape
    cells = n_img * BRICK_DEV * weights.shape[0]
    tiles_ref = images.shape[1] // weights.shape[1]
    room = 2 * (images.size + rows * depth * n_img * (1 + cells // weights.shape[1]))
    fits = (
        depth % LANES == 0
        and 2 * (rows // n_img) == LANES
        and LANES % tiles_ref == 0
        and tiles_ref % 32 == 0
        and cells <= PACK // 2
        and lax.axis_size("ori") == 2 * CORES
        and rows * tiles_ref == 16 * LANES * n_img
        and n_img % (2 * NY) == 0
        and n_img >= 4 * NY
        and room < 48 * 2**20
    )
    return fused_body(*args) if fits else plain_body(*args)


def solution(mesh):
    placed = (
        P("img", None),
        P("img"),
        P("ori", "img"),
        P("img", "ori"),
        P("ori", "img", None),
        P("ori", "img"),
        P("ori", "img"),
        P(),
    )
    return jax.shard_map(
        body,
        mesh=mesh,
        in_specs=placed,
        out_specs=(P(("img", "ori"), None), P("img")),
        check_vma=False,
    )
```

```python
import functools
import math

import jax
import jax.numpy as jnp
from jax import lax
from jax.experimental import pallas as pl
from jax.experimental.pallas import tpu as pltpu
from jax.sharding import PartitionSpec as P

BRICK_DEV = 16
LANES = 128
NY = 2
PARTS = 2
CORES = 2
PACK = 1 << 16
F8 = jnp.float8_e4m3fn
TOP = 256.0
LOW = 32.0
MESH = pl.DeviceIdType.MESH


def plain_body(
    images, img_scale, references, pattern, tile_owner, tile_brick, tile_block, distance_weights
):
    image_rows, width = images.shape
    ref_local = references.shape[0]
    group_size = ref_local // pattern.shape[1]
    positions, tile_width, voxels = distance_weights.shape
    inv_root = 1.0 / math.sqrt(width)
    weight_table = distance_weights.astype(jnp.float32)
    raw_scores = lax.dot_general(
        images,
        lax.all_gather(references, "img", axis=1, tiled=True),
        (((1,), (1,)), ((), ())),
        preferred_element_type=jnp.float32,
    )
    scores = raw_scores * img_scale[:, None] * inv_root
    active = jnp.repeat(pattern > 0, group_size, axis=1)
    masked = jnp.where(active, scores, -1e30)
    local_peak = jnp.max(masked, axis=1)
    peak = lax.pmax(local_peak, "ori")
    expo = jnp.where(active, jnp.exp(masked - peak[:, None]), 0.0)
    mass = lax.psum(jnp.sum(expo, axis=1), "ori")
    weights = expo / mass[:, None]
    log_evidence = peak + jnp.log(mass)
    scaled = (weights * img_scale[:, None]).astype(jnp.bfloat16)
    partial_value = lax.dot_general(
        scaled, images, (((0,), (0,)), ((), ())), preferred_element_type=jnp.float32
    )
    owners = tile_owner.reshape(-1)
    local_code = tile_brick.reshape(-1) * positions + tile_block.reshape(-1)
    cells = BRICK_DEV * positions
    tile_code = owners * cells + local_code
    group_code = lax.all_gather(tile_code, "img", axis=0, tiled=True)
    peers = lax.axis_size("img")
    group_tiles = partial_value.reshape(-1, tile_width)
    collected = jax.ops.segment_sum(group_tiles, group_code, num_segments=peers * cells)
    brick_terms = jnp.einsum(
        "bpt,ptv->bv",
        collected.reshape(peers * BRICK_DEV, positions, tile_width),
        weight_table,
        precision=lax.Precision.HIGHEST,
    )
    bricks = lax.psum_scatter(brick_terms, ("img", "ori"), scatter_dimension=0, tiled=True)
    return (bricks, log_evidence)


def kernel(
    n_img, n_ori, tiles_ref, inv_root,
    refs, images, scale, pattern, owner, brick_of, block_of, weights,
    sums_out, stats_out,
    img_v, buf, w_v, sc, scaled, codes, codes_buf, codes_all, onehot, rhs_a, rhs_b, acc,
    halves, stats, stats_buf, terms, terms_buf, mid, mid_buf,
    img_sem, w_sem, own_sem, up_sem, dn_sem, y_sem, recv_sem, code_send, code_recv,
    stat_send, stat_recv, a_send, a_recv, b_send, b_recv, hop_sem,
):
    nz = n_img // NY
    me = lax.axis_index("img")
    ori = lax.axis_index("ori")
    z, y = me // NY, me % NY
    zp = z + 1 - 2 * (z % 2)
    rows, depth = refs.shape
    half = rows // 2
    quarter = rows // PARTS
    n_images = img_v.shape[1]
    groups = pattern.shape[0]
    group = rows // groups
    tile_width, (depth_w, voxels) = acc.shape[1] // 2, w_v.shape
    positions = depth_w // tile_width
    chunk_tiles = depth // tile_width
    cells = acc.shape[0]

    def image_copy(f):
        return pltpu.make_async_copy(
            images.at[:, pl.ds(f * depth, depth)], img_v.at[f], img_sem.at[f]
        )

    w_copy = pltpu.make_async_copy(weights, w_v, w_sem)
    own_copy = pltpu.make_async_copy(refs, buf.at[me], own_sem)

    up, dn, yn = me + NY, me - NY, z * NY + 1 - y
    has_up, has_dn = z < nz - 1, z > 0
    near = 1 + has_up.astype(jnp.int32) + has_dn.astype(jnp.int32)

    def greet(sem):
        @pl.when(has_up)
        def _():
            pl.semaphore_signal(sem, inc=1, device_id=(up, ori), device_id_type=MESH)

        @pl.when(has_dn)
        def _():
            pl.semaphore_signal(sem, inc=1, device_id=(dn, ori), device_id_type=MESH)

        pl.semaphore_signal(sem, inc=1, device_id=(yn, ori), device_id_type=MESH)

    barrier = pltpu.get_barrier_semaphore()
    greet(barrier)
    for step in range(1, n_ori):
        pl.semaphore_signal(
            barrier, inc=1, device_id=(me, (ori + step) % n_ori), device_id_type=MESH
        )
    per = rows // n_img
    th = tiles_ref // 2
    lines = BRICK_DEV // n_ori
    brick_ids = brick_of[...]
    place_of = brick_ids // lines
    raw = (
        (place_of // CORES) * (cells // (n_ori // CORES))
        + block_of[...] * (CORES * n_img * lines)
        + (place_of % CORES) * (n_img * lines)
        + owner[...] * lines
        + brick_ids % lines
    )
    held_rows = raw.shape[0]
    turned = jnp.concatenate(
        [raw, jnp.zeros((LANES - held_rows, LANES), jnp.int32)], axis=0
    ).T
    local = jnp.zeros((tiles_ref, LANES), jnp.int32)
    for j in range(LANES // tiles_ref):
        cut = turned[j * tiles_ref:(j + 1) * tiles_ref, :]
        local += pltpu.roll(cut, j * held_rows, 1) if j else cut
    wide = local[0:th, :] + pltpu.roll(local[th:, :], per, 1)
    codes[...] = wide[0:th // 2, :] + wide[th // 2:, :] * PACK

    pl.semaphore_wait(barrier, near + n_ori - 1)

    def code_copy(step):
        return pltpu.make_async_remote_copy(
            src_ref=codes,
            dst_ref=codes_buf.at[me],
            send_sem=code_send.at[step],
            recv_sem=code_recv.at[me],
            device_id=((me + step) % n_img, ori),
            device_id_type=MESH,
        )

    def code_arrival(step):
        other = (me + step) % n_img
        return pltpu.make_async_remote_copy(
            src_ref=codes,
            dst_ref=codes_buf.at[other],
            send_sem=code_send.at[step],
            recv_sem=code_recv.at[other],
            device_id=(other, ori),
            device_id_type=MESH,
        )

    def piece(src, sl, q, sems, to):
        return pltpu.make_async_remote_copy(
            src_ref=src,
            dst_ref=buf.at[sl, pl.ds(pl.multiple_of(q * quarter, quarter), quarter), :],
            send_sem=sems.at[sl * PARTS + q],
            recv_sem=recv_sem.at[sl * PARTS + q],
            device_id=(to, ori),
            device_id_type=MESH,
        )

    def held(sl, q):
        return buf.at[sl, pl.ds(pl.multiple_of(q * quarter, quarter), quarter), :]

    for h in range(PARTS):
        own = refs.at[pl.ds(h * quarter, quarter), :]

        @pl.when(has_up)
        def _():
            piece(own, me, h, up_sem, up).start()

        @pl.when(has_dn)
        def _():
            piece(own, me, h, dn_sem, dn).start()

        piece(own, me, h, y_sem, yn).start()

    own_copy.start()
    for f in range(n_img):
        image_copy(f).start()
    w_copy.start()
    for hop in range(nz - 1):
        greet(hop_sem.at[hop])
        pl.semaphore_wait(hop_sem.at[hop], near)
    for step in range(1, n_img):
        code_copy(step).start()

    codes_buf[me] = codes[...]
    sc[...] = jnp.zeros_like(sc)
    acc[...] = jnp.zeros_like(acc)
    own_copy.wait()
    for f in range(n_img):
        image_copy(f).wait()

    def brightest(i, top):
        f, at = i // (n_images // 16), pl.multiple_of((i % (n_images // 16)) * 16, 16)
        return jnp.maximum(top, jnp.abs(img_v[f, pl.ds(at, 16), :]))

    bright = lax.fori_loop(
        0, n_img * n_images // 16, brightest, jnp.zeros((16, depth), jnp.bfloat16)
    )
    bright = jnp.max(bright.astype(jnp.float32), axis=(0, 1), keepdims=True)

    def spread_codes():
        for step in range(1, n_img):
            code_arrival(step).wait_recv()
        low = lax.broadcasted_iota(jnp.int32, (th, LANES), 1) < per

        def unpacked(i):
            two = codes_buf[i]
            return jnp.concatenate([two % PACK, two // PACK], axis=0)

        for j in range(n_img // 2):
            a, b = unpacked(2 * j), unpacked(2 * j + 1)
            cut = slice(j * LANES, (j + 1) * LANES)
            codes_all[0:th, cut] = jnp.where(low, a, pltpu.roll(b, per, 1))
            codes_all[th:, cut] = jnp.where(low, pltpu.roll(a, per, 1), b)

    def place(s):
        r, q, k = s // (4 * PARTS), (s // 4) % PARTS, s % 4
        far = q >= PARTS // 2
        other = k // 2
        dist = r - other
        below = (k % 2) == 0
        slz = jnp.where(below, z - dist, z + dist)
        late = jnp.logical_and(jnp.logical_and(r == nz, far), k == 1)
        ok = jnp.logical_and(slz >= 0, slz < nz)
        ok = jnp.logical_and(ok, dist >= jnp.where(below, 0, 1))
        ok = jnp.logical_and(ok, dist < nz)
        skipped = jnp.logical_and(slz == zp, far)
        ok = jnp.logical_and(
            ok, jnp.logical_not(jnp.logical_and(other == 1, skipped))
        )
        ok = jnp.logical_or(ok, late)
        slz = jnp.where(late, zp, slz)
        sl = jnp.where(jnp.logical_or(other == 1, late), slz * NY + 1 - y, slz * NY + y)
        moving = jnp.logical_and(jnp.logical_and(other == 0, r > 0), jnp.logical_not(late))
        moving = jnp.logical_and(moving, ok)
        go_up = jnp.logical_and(jnp.logical_and(moving, below), has_up)
        go_dn = jnp.logical_and(jnp.logical_and(moving, jnp.logical_not(below)), has_dn)
        go_y = jnp.logical_and(moving, jnp.logical_not(skipped))
        sl = jnp.where(ok, sl, me)
        return r, q, k, sl, ok, go_up, go_dn, go_y

    steps = (nz + 1) * 4 * PARTS
    late_sl = z * NY + 1 - y

    strip = 16
    n_strips = half // strip
    factor = scale[...] * inv_root

    blocks = n_images // LANES

    def score_rows(at):
        return jnp.concatenate([sc[c, at, :] for c in range(blocks)], axis=1)

    def keep_rows(at, value):
        for c in range(blocks):
            sc[c, at, :] = value[:, c * LANES:(c + 1) * LANES]

    def half_softmax(h):
        def at_strip(i):
            i = h * n_strips + i
            flag = pattern[pl.ds(i // (group // strip), 1), :] > 0
            return pl.ds(pl.multiple_of(i * strip, strip), strip), flag

        def peak_of(i, m):
            at, flag = at_strip(i)
            s = jnp.where(flag, score_rows(at) * factor, -1e30)
            keep_rows(at, s)
            return jnp.maximum(m, s)

        m = lax.fori_loop(
            0, n_strips, peak_of, jnp.full((strip, n_images), -1e30, jnp.float32), unroll=2
        )
        m = jnp.max(m, axis=0, keepdims=True)

        def mass_of(i, t):
            at, flag = at_strip(i)
            e = jnp.where(flag, jnp.exp(score_rows(at) - m), 0.0)
            keep_rows(at, e)
            return t + e

        t = lax.fori_loop(
            0, n_strips, mass_of, jnp.zeros((strip, n_images), jnp.float32), unroll=2
        )
        halves[2 * h:2 * h + 1, :] = m
        halves[2 * h + 1:2 * h + 2, :] = jnp.sum(t, axis=0, keepdims=True)

    first_hot = 2 * 4 * PARTS

    def arrive(s, carry):
        r, q, k, sl, ok, go_up, go_dn, go_y = place(s)

        @pl.when(s == (nz * PARTS + PARTS // 2) * 4)
        def _():
            half_softmax(0)

        @pl.when(s == first_hot)
        def _():
            spread_codes()

        @pl.when(jnp.logical_and(ok, r + k > 0))
        def _():
            piece(held(sl, q), sl, q, y_sem, yn).wait_recv()

        @pl.when(go_up)
        def _():
            piece(held(sl, q), sl, q, up_sem, up).start()

        @pl.when(go_dn)
        def _():
            piece(held(sl, q), sl, q, dn_sem, dn).start()

        @pl.when(go_y)
        def _():
            piece(held(sl, q), sl, q, y_sem, yn).start()

        turn = jnp.logical_and(r == nz - 1, jnp.logical_and(q == 0, k == 0))

        @pl.when(jnp.logical_and(turn, zp > z))
        def _():
            for late_q in range(PARTS // 2, PARTS):
                piece(held(late_sl, late_q), late_sl, late_q, up_sem, up).start()

        @pl.when(jnp.logical_and(turn, zp < z))
        def _():
            for late_q in range(PARTS // 2, PARTS):
                piece(held(late_sl, late_q), late_sl, late_q, dn_sem, dn).start()

        @pl.when(jnp.logical_and(ok, (q + 1) % (PARTS // 2) == 0))
        def _():
            at = pl.ds(pl.multiple_of((q // (PARTS // 2)) * half, half), half)
            term = lax.dot_general(
                buf[sl, at, :], img_v[sl], (((1,), (1,)), ((), ())),
                preferred_element_type=jnp.float32,
            )
            for c in range(blocks):
                sc[c, at, :] += term[:, c * LANES:(c + 1) * LANES]

        @pl.when(jnp.logical_and(s >= first_hot, s < first_hot + tiles_ref // 2))
        def _():
            for u in range(2):
                tile = 2 * (s - first_hot) + u
                code = codes_all[pl.ds(tile, 1), :]
                f, q = tile // chunk_tiles, tile % chunk_tiles
                at = pl.ds(pl.multiple_of(q * rows, rows), rows)

                def part(i, c):
                    base = pl.multiple_of(i * 64, 64)
                    row = lax.broadcasted_iota(jnp.int32, (64, rows), 0) + base
                    onehot[f, pl.ds(base, 64), at] = jnp.where(row == code, 1.0, 0.0).astype(
                        F8
                    )
                    return c

                lax.fori_loop(0, cells // 64, part, 0)

        return carry

    lax.fori_loop(0, steps, arrive, 0)

    half_softmax(1)
    m = jnp.maximum(halves[0:1, :], halves[2:3, :])
    total = halves[1:2, :] * jnp.exp(halves[0:1, :] - m)
    total += halves[3:4, :] * jnp.exp(halves[2:3, :] - m)
    stats[0:1, :] = m
    stats[1:2, :] = total

    def stat_copy(step, slot):
        return pltpu.make_async_remote_copy(
            src_ref=stats,
            dst_ref=stats_buf.at[slot],
            send_sem=stat_send.at[step],
            recv_sem=stat_recv.at[slot],
            device_id=(me, (ori + step) % n_ori),
            device_id_type=MESH,
        )

    for step in range(1, n_ori):
        stat_copy(step, ori).start()
    peak = m
    for step in range(1, n_ori):
        slot = (ori + step) % n_ori
        stat_copy(step, slot).wait_recv()
        peak = jnp.maximum(peak, stats_buf[slot, 0:1, :])
    mass = total * jnp.exp(m - peak)
    for step in range(1, n_ori):
        slot = (ori + step) % n_ori
        mass += stats_buf[slot, 1:2, :] * jnp.exp(stats_buf[slot, 0:1, :] - peak)
    stats_out[0:1, :] = peak
    stats_out[1:2, :] = mass
    share_of = scale[...] / mass

    spread = LANES // tiles_ref
    power = jnp.zeros((strip, LANES), jnp.float32)
    for h in range(2):
        weight = jnp.exp(halves[2 * h:2 * h + 1, :] - peak) * share_of

        def scale_of(i, top):
            i = h * n_strips + i
            first = (i // spread) * per + i % spread
            at = pl.ds(pl.multiple_of(i * strip, strip), strip)
            value = score_rows(pl.ds(first, strip, stride=spread)) * weight
            scaled[at, :] = value.astype(jnp.bfloat16)
            square = value * value
            held = square[:, 0:LANES]
            for c in range(1, blocks):
                held += square[:, c * LANES:(c + 1) * LANES]
            return jnp.maximum(top, held)

        power = lax.fori_loop(0, n_strips, scale_of, power, unroll=2)
    power = jnp.max(jnp.sum(power, axis=1, keepdims=True), axis=0, keepdims=True)
    largest = jnp.maximum(jnp.sqrt(power), 1e-15)
    largest = largest * (math.sqrt(n_images) * jnp.maximum(bright, 1e-18))
    grow, shrink = TOP / largest, largest * (1.0 / TOP)

    def values(f, j, rhs):
        value = jnp.dot(scaled[...], img_v[f], preferred_element_type=jnp.float32) * grow
        hi = value.astype(F8)
        lo = ((value - hi.astype(jnp.float32)) * LOW).astype(F8)
        for q in range(chunk_tiles):
            cut = slice(q * tile_width, (q + 1) * tile_width)
            rhs[j, q * rows:(q + 1) * rows, 0:tile_width] = hi[:, cut]
            rhs[j, q * rows:(q + 1) * rows, tile_width:] = lo[:, cut]

    x_me, core = ori // CORES, ori % CORES
    chips = n_ori // CORES
    side = cells // chips
    share = n_img * lines

    def collect(f, j, rhs, chip):
        at = pl.ds(pl.multiple_of(chip * side, side), side)
        acc[at, :] += jnp.dot(onehot[f, at, :], rhs[j], preferred_element_type=jnp.float32)

    def brick_terms(chip):
        at = pl.ds(pl.multiple_of(chip * side, side), side)
        both = acc[at, :]
        c = (both[:, 0:tile_width] + both[:, tile_width:] * (1.0 / LOW)) * shrink
        hi = c.astype(jnp.bfloat16)
        lo = (c - hi.astype(jnp.float32)).astype(jnp.bfloat16)
        n = side // positions
        wide_hi = jnp.concatenate([hi[p * n:(p + 1) * n, :] for p in range(positions)], axis=1)
        wide_lo = jnp.concatenate([lo[p * n:(p + 1) * n, :] for p in range(positions)], axis=1)
        wide = jnp.concatenate([wide_hi, wide_lo], axis=0)
        brick = jnp.dot(wide, w_v[...], preferred_element_type=jnp.float32)
        brick = brick[0:n, :] + brick[n:, :]
        for c in range(CORES):
            terms[chip * CORES + c] = brick[c * share:(c + 1) * share, :]

    def term_copy(to, slot):
        return pltpu.make_async_remote_copy(
            src_ref=terms.at[to],
            dst_ref=terms_buf.at[slot],
            send_sem=a_send.at[to],
            recv_sem=a_recv.at[slot],
            device_id=(me, to),
            device_id_type=MESH,
        )

    values(0, 0, rhs_a)

    def first_side(j, c):
        values(2 * j + 1, j, rhs_b)
        collect(2 * j, j, rhs_a, 1 - x_me)
        values(2 * j + 2, j + 1, rhs_a)
        collect(2 * j + 1, j, rhs_b, 1 - x_me)
        return c

    last = n_img // 2 - 1
    lax.fori_loop(0, last, first_side, 0)
    values(n_img - 1, last, rhs_b)
    collect(n_img - 2, last, rhs_a, 1 - x_me)
    collect(n_img - 1, last, rhs_b, 1 - x_me)
    w_copy.wait()
    brick_terms(1 - x_me)
    for c in range(CORES):
        term_copy((1 - x_me) * CORES + c, ori).start()

    def second_side(j, c):
        collect(2 * j, j, rhs_a, x_me)
        collect(2 * j + 1, j, rhs_b, x_me)
        return c

    lax.fori_loop(0, n_img // 2, second_side, 0)
    brick_terms(x_me)
    mate = x_me * CORES + 1 - core
    term_copy(mate, ori).start()
    mine = terms[ori]
    term_copy(mate, mate).wait_recv()
    mine += terms_buf[mate]
    for c in range(CORES):
        slot = (1 - x_me) * CORES + c
        term_copy(slot, slot).wait_recv()
        mine += terms_buf[slot]
    for i in range(n_img):
        mid[i] = mine[i * lines:(i + 1) * lines, :]

    def mid_copy(step, slot):
        to = (me + step) % n_img
        return pltpu.make_async_remote_copy(
            src_ref=mid.at[to],
            dst_ref=mid_buf.at[slot],
            send_sem=b_send.at[step],
            recv_sem=b_recv.at[slot],
            device_id=(to, ori),
            device_id_type=MESH,
        )

    for step in range(1, n_img):
        mid_copy(step, me).start()
    for step in range(1, n_img):
        code_copy(step).wait_send()
    for step in range(1, n_ori):
        stat_copy(step, ori).wait_send()
        term_copy((ori + step) % n_ori, ori).wait_send()
    for h in range(PARTS):
        own = refs.at[pl.ds(h * quarter, quarter), :]

        @pl.when(has_up)
        def _():
            piece(own, me, h, up_sem, up).wait_send()

        @pl.when(has_dn)
        def _():
            piece(own, me, h, dn_sem, dn).wait_send()

        piece(own, me, h, y_sem, yn).wait_send()

    @pl.when(zp > z)
    def _():
        for late_q in range(PARTS // 2, PARTS):
            piece(held(late_sl, late_q), late_sl, late_q, up_sem, up).wait_send()

    @pl.when(zp < z)
    def _():
        for late_q in range(PARTS // 2, PARTS):
            piece(held(late_sl, late_q), late_sl, late_q, dn_sem, dn).wait_send()

    def drain(s, carry):
        r, q, k, sl, ok, go_up, go_dn, go_y = place(s)

        @pl.when(go_up)
        def _():
            piece(held(sl, q), sl, q, up_sem, up).wait_send()

        @pl.when(go_dn)
        def _():
            piece(held(sl, q), sl, q, dn_sem, dn).wait_send()

        @pl.when(go_y)
        def _():
            piece(held(sl, q), sl, q, y_sem, yn).wait_send()

        return carry

    lax.fori_loop(0, steps, drain, 0)

    result = mid[me]
    for step in range(1, n_img):
        slot = (me + step) % n_img
        mid_copy(step, slot).wait_recv()
        if step < n_img - 1:
            result += mid_buf[slot]
    sums_out[0] = result
    sums_out[1] = mid_buf[(me + n_img - 1) % n_img]
    for step in range(1, n_img):
        mid_copy(step, me).wait_send()


def finish(sums, stats, bricks, evidence):
    bricks[...] = sums[0] + sums[1]
    evidence[...] = stats[0:1, :] + jnp.log(stats[1:2, :])


def fused_body(
    images, img_scale, references, pattern, tile_owner, tile_brick, tile_block, distance_weights
):
    n_img, n_ori = lax.axis_size("img"), lax.axis_size("ori")
    n_images, width = images.shape
    rows, depth = references.shape
    positions, tile_width, voxels = distance_weights.shape
    tiles_ref = width // tile_width
    lines = BRICK_DEV // n_ori
    cells = n_img * BRICK_DEV * positions
    flat = (tile_brick.size // LANES, LANES)
    bf16, f32, i32 = jnp.bfloat16, jnp.float32, jnp.int32
    vmem = pl.BlockSpec(memory_space=pltpu.VMEM)
    hbm = pl.BlockSpec(memory_space=pl.ANY)
    dma = pltpu.SemaphoreType.DMA
    sums, stats = pl.pallas_call(
        functools.partial(kernel, n_img, n_ori, tiles_ref, 1.0 / math.sqrt(width)),
        out_shape=(
            jax.ShapeDtypeStruct((2, lines, voxels), f32),
            jax.ShapeDtypeStruct((2, n_images), f32),
        ),
        in_specs=[hbm, hbm, vmem, vmem, vmem, vmem, vmem, hbm],
        out_specs=(vmem, vmem),
        scratch_shapes=[
            pltpu.VMEM((n_img, n_images, depth), bf16),
            pltpu.VMEM((n_img, rows, depth), bf16),
            pltpu.VMEM((positions * tile_width, voxels), bf16),
            pltpu.VMEM((n_images // LANES, rows, LANES), f32),
            pltpu.VMEM((rows, n_images), bf16),
            pltpu.VMEM((tiles_ref // 4, LANES), i32),
            pltpu.VMEM((n_img, tiles_ref // 4, LANES), i32),
            pltpu.VMEM((tiles_ref, rows), i32),
            pltpu.VMEM((n_img, cells, rows * depth // tile_width), F8),
            pltpu.VMEM((n_img // 2, rows * depth // tile_width, 2 * tile_width), F8),
            pltpu.VMEM((n_img // 2, rows * depth // tile_width, 2 * tile_width), F8),
            pltpu.VMEM((cells, 2 * tile_width), f32),
            pltpu.VMEM((4, n_images), f32),
            pltpu.VMEM((2, n_images), f32),
            pltpu.VMEM((n_ori, 2, n_images), f32),
            pltpu.VMEM((n_ori, n_img * lines, voxels), f32),
            pltpu.VMEM((n_ori, n_img * lines, voxels), f32),
            pltpu.VMEM((n_img, lines, voxels), f32),
            pltpu.VMEM((n_img, lines, voxels), f32),
            dma((n_img,)),
            dma,
            dma,
            dma((PARTS * n_img,)),
            dma((PARTS * n_img,)),
            dma((PARTS * n_img,)),
            dma((PARTS * n_img,)),
            dma((n_img,)),
            dma((n_img,)),
            dma((n_ori,)),
            dma((n_ori,)),
            dma((n_ori,)),
            dma((n_ori,)),
            dma((n_img,)),
            dma((n_img,)),
            pltpu.SemaphoreType.REGULAR((n_img // NY - 1,)),
        ],
        compiler_params=pltpu.CompilerParams(
            collective_id=0, has_side_effects=True, vmem_limit_bytes=67043328
        ),
    )(
        references,
        images,
        img_scale[None, :],
        pattern.T,
        tile_owner.reshape(flat),
        tile_brick.reshape(flat),
        tile_block.reshape(flat),
        distance_weights.reshape(positions * tile_width, voxels),
    )
    bricks, evidence = pl.pallas_call(
        finish,
        out_shape=(
            jax.ShapeDtypeStruct((lines, voxels), f32),
            jax.ShapeDtypeStruct((1, n_images), f32),
        ),
        in_specs=[vmem, vmem],
        out_specs=(vmem, vmem),
    )(sums, stats)
    return bricks, evidence.reshape(-1)


def body(*args):
    images, references, weights = args[0], args[2], args[7]
    n_img = lax.axis_size("img")
    rows, depth = references.shape
    cells = n_img * BRICK_DEV * weights.shape[0]
    tiles_ref = images.shape[1] // weights.shape[1]
    room = 2 * (images.size + rows * depth * n_img * (1 + cells // weights.shape[1]))
    fits = (
        depth % LANES == 0
        and 2 * (rows // n_img) == LANES
        and LANES % tiles_ref == 0
        and tiles_ref % 32 == 0
        and cells <= PACK // 2
        and lax.axis_size("ori") == 2 * CORES
        and rows * tiles_ref == 16 * LANES * n_img
        and n_img % (2 * NY) == 0
        and n_img >= 4 * NY
        and room < 48 * 2**20
    )
    return fused_body(*args) if fits else plain_body(*args)


def solution(mesh):
    placed = (
        P("img", None),
        P("img"),
        P("ori", "img"),
        P("img", "ori"),
        P("ori", "img", None),
        P("ori", "img"),
        P("ori", "img"),
        P(),
    )
    return jax.shard_map(
        body,
        mesh=mesh,
        in_specs=placed,
        out_specs=(P(("img", "ori"), None), P("img")),
        check_vma=False,
    )
```
